512 devices in a mesh: tok: 8 (over z), wid: 64 (over x, y, core).
Axes of the slice: x: 4, y: 8, z: 8, core: 2. Of those that a mesh axis runs over, the one named last changes fastest.
Arguments:
- tokens: bfloat16 [1536, 4096], P('tok', 'wid'), may hold values from -80 to 80
- gate_a: bfloat16 [16384, 4096], P('wid', 'tok'), may hold values from -0.09375 to 0.09375
- up_a: bfloat16 [16384, 4096], P('wid', 'tok'), may hold values from -0.09375 to 0.09375
- gate_b: bfloat16 [16384, 4096], P('wid', 'tok'), may hold values from -0.09375 to 0.09375
- up_b: bfloat16 [16384, 4096], P('wid', 'tok'), may hold values from -0.09375 to 0.09375
- down_a: bfloat16 [16384, 4096], P('wid', 'tok'), may hold values from -0.125 to 0.125
- down_b: bfloat16 [16384, 4096], P('wid', 'tok'), may hold values from -0.125 to 0.125
- block_perm: int32 [128], replicated, may hold values from 0 to 127, each once
Outputs:
- merged: bfloat16 [1536, 4096], P('tok', 'wid')
The draws below stay inside these ranges and needn't reach their ends.
Inputs may be any that keep to these rules, and one draw needn't show every extreme that they name: block_perm names every block number once.
All inputs are finite; a program needn't handle non-finite values.
Results may differ from the reference program's by a relative error of at most 0.0058.
Values may be sent and summed in bfloat16 or wider, within the bound.
A program may use at most 64 MiB of HBM per device.

```python
import jax
import jax.numpy as jnp
from jax import lax

D = 4096
FF = 16384
BLOCK = 128
TOKENS = 1536
NB = 128


def draw_tokens(key, part):
    key_base, key_rows, key_cols = jax.random.split(key, 3)
    positions = jnp.arange(TOKENS, dtype=jnp.float32)
    rising = 0.5 + positions / (TOKENS - 1)
    base = jnp.clip(jax.random.normal(key_base, (TOKENS, D), jnp.float32), -5.0, 5.0)
    row_scale = 10.0 ** (jax.random.uniform(key_rows, (TOKENS, 1), jnp.float32) - 0.5) * rising[:, None]
    col_scale = 10.0 ** (jax.random.uniform(key_cols, (1, D), jnp.float32) - 0.5)
    return (base * row_scale * col_scale).astype(jnp.bfloat16)


def spiked(result, stream_key, source, target, parts, factor):
    def block_of(axis_at):
        return (jnp.arange(result.shape[axis_at]) // (result.shape[axis_at] // parts)).reshape((-1,) + (1,) * (result.ndim - 1 - axis_at))

    near = jax.random.permutation(stream_key, parts)[block_of(target)]
    second = (block_of(target) + parts // 2) % parts
    return jnp.where((block_of(source) == near) | (block_of(source) == second), factor * result, result)


def block_scale(stream_key, dims, shards, least, high):
    loudness, own = 1.0, jax.random.fold_in(stream_key, 6)
    for axis_at, shards_of in shards:
        steps = jnp.exp(jax.random.uniform(jax.random.fold_in(own, axis_at), (shards_of,), jnp.float32, least / len(shards), high / len(shards)))
        loudness = loudness * jnp.repeat(steps, dims[axis_at] // shards_of).reshape([-1 if axis == axis_at else 1 for axis in range(len(dims))])
    return loudness


def normal_values(rng, extent, deviation, most, cuts=(), held_as=jnp.bfloat16):
    array = deviation * jax.random.normal(rng, extent, jnp.float32)
    if cuts:
        array = array * block_scale(rng, extent, cuts, -0.22, 0.18)
    return jnp.clip(array, -most, most).astype(held_as)


def bell_draw_with(stream_key, extent, width, bound, pieces, heavy, kind=jnp.bfloat16):
    values = width * jax.random.normal(stream_key, extent, jnp.float32)
    if pieces:
        values = values * block_scale(stream_key, extent, pieces, -0.22, 0.18)
    return jnp.clip(spiked(values, jax.random.fold_in(stream_key, 3), *heavy), -bound, bound).astype(kind)


def setup_inputs(seed: int = 0) -> dict:
    streams_of = jax.random.split(jax.random.key(seed), 9)
    tokens = draw_tokens(jax.random.fold_in(streams_of[8], 71), 0)
    gate_a = normal_values(streams_of[1], (FF, D), D ** -0.5, 0.09375, ((0, 64), (1, 8)))
    up_a = normal_values(streams_of[2], (FF, D), D ** -0.5, 0.09375, ((0, 64), (1, 8)))
    gate_b = normal_values(streams_of[3], (FF, D), D ** -0.5, 0.09375, ((0, 64), (1, 8)))
    up_b = normal_values(streams_of[4], (FF, D), D ** -0.5, 0.09375, ((0, 64), (1, 8)))
    down_a = bell_draw_with(streams_of[5], (FF, D), FF ** -0.5, 0.125, ((0, 64), (1, 8)), (0, 1, 64, 4.0))
    down_b = bell_draw_with(streams_of[6], (FF, D), FF ** -0.5, 0.125, ((0, 64), (1, 8)), (0, 1, 64, 4.0))
    block_perm = jax.random.permutation(streams_of[7], NB).astype(jnp.int32)
    return {"tokens": tokens, "gate_a": gate_a, "up_a": up_a, "gate_b": gate_b, "up_b": up_b, "down_a": down_a, "down_b": down_b, "block_perm": block_perm}


def sigmoid_linear(preact):
    return preact / (1.0 + jnp.exp(-preact))

def reorder_blocks(matrix_in, block_perm):
    shaped = matrix_in.reshape(matrix_in.shape[0] // BLOCK, BLOCK, matrix_in.shape[1])
    return jnp.take(shaped, block_perm, axis=0).reshape(matrix_in.shape)

def project_rows(tokens, weight):
    return jnp.dot(tokens, weight.T, preferred_element_type=jnp.float32)

def unit_stats(hidden):
    center = lax.optimization_barrier(jnp.mean(hidden, axis=0))
    spread = lax.optimization_barrier(jnp.mean((hidden - center) ** 2, axis=0))
    return (center, jnp.sqrt(spread + 1e-05))

def reference(tokens, gate_a, up_a, gate_b, up_b, down_a, down_b, block_perm):
    gate_av = project_rows(tokens, gate_a)
    up_av = project_rows(tokens, up_a)
    gate_bv = project_rows(tokens, reorder_blocks(gate_b, block_perm))
    up_bv = project_rows(tokens, reorder_blocks(up_b, block_perm))
    hid_a = sigmoid_linear(gate_av) * up_av
    hid_b = sigmoid_linear(gate_bv) * up_bv
    hid_m = sigmoid_linear(0.5 * (gate_av + gate_bv)) * (0.5 * (up_av + up_bv))
    center_a, dev_a = unit_stats(hid_a)
    center_b, dev_b = unit_stats(hid_b)
    center_m, dev_m = unit_stats(hid_m)
    target_std = 0.5 * (dev_a + dev_b)
    target_mean = 0.5 * (center_a + center_b)
    repaired = ((hid_m - center_m) / dev_m * target_std + target_mean).astype(jnp.bfloat16)
    down_perm = reorder_blocks(down_b, block_perm)
    down_mid = ((down_a.astype(jnp.float32) + down_perm.astype(jnp.float32)) * 0.5).astype(jnp.bfloat16)
    return jnp.dot(repaired, down_mid, preferred_element_type=jnp.float32).astype(jnp.bfloat16)
```

```python
import functools

import jax
import jax.numpy as jnp
from jax import lax
from jax.experimental import pallas as pl
from jax.experimental.pallas import tpu as pltpu
from jax.sharding import PartitionSpec as P

NB = 128
GROUPS = 4
F32 = jnp.float32
BF16 = jnp.bfloat16
MESH_IDS = pl.DeviceIdType.MESH
VMEM_BYTES = 56 * 1024 * 1024


def copy_to(src, dst, send, recv, z, w):
    return pltpu.make_async_remote_copy(
        src_ref=src, dst_ref=dst, send_sem=send, recv_sem=recv, device_id=(z, w), device_id_type=MESH_IDS
    )


def signal(sem, z, w):
    pl.semaphore_signal(sem, inc=1, device_id=(z, w), device_id_type=MESH_IDS)


def position():
    z, w = lax.axis_index("tok"), lax.axis_index("wid")
    return z, w, w // 16, (w // 2) % 8, w % 2


def piece_of(x, y, c):
    return 4 * x + y // 2, 2 * c + y % 2


def piece_home(z, w, h):
    m = (w % 8) // 2
    return w // 8, 4 * (2 * z + h) + 2 * (m % 2) + m // 2


def greet(barrier, z, w, x, y, c, others):
    for k in range(1, 8):
        signal(barrier, z, 16 * x + 2 * ((y + k) % 8) + c)
    for k in range(1, 4):
        signal(barrier, z, 16 * ((x + k) % 4) + 2 * y + c)
    signal(barrier, z, 16 * x + 2 * y + (1 - c))
    own = 0
    for oz, ow in others:
        same = jnp.logical_and(oz == z, ow == w)
        own = own + same.astype(jnp.int32)

        @pl.when(jnp.logical_not(same))
        def _():
            signal(barrier, oz, ow)

    pl.semaphore_wait(barrier, 13 - own)


def either_start(src, dst, send, recv, z, w, oz, ow):
    same = jnp.logical_and(oz == z, ow == w)

    @pl.when(same)
    def _():
        pltpu.make_async_copy(src, dst, recv).start()

    @pl.when(jnp.logical_not(same))
    def _():
        copy_to(src, dst, send, recv, oz, ow).start()


def either_wait_send(src, dst, send, recv, z, w, oz, ow):
    same = jnp.logical_and(oz == z, ow == w)

    @pl.when(jnp.logical_not(same))
    def _():
        copy_to(src, dst, send, recv, oz, ow).wait_send()


def tokens_kernel(t_ref, x_ref, landed, piece, send, recv, local_sem):
    z, w, x, y, c = position()
    q, m = piece_of(x, y, c)
    e = w % 2
    barrier = pltpu.get_barrier_semaphore()
    sources = [(q // 2, 8 * z + 2 * m + s) for s in range(2)]
    homes = [piece_home(z, w, h) for h in range(2)]
    greet(barrier, z, w, x, y, c, sources)
    for h in range(2):
        either_start(t_ref.at[h], landed.at[e], send.at[h], recv.at[e], z, w, *homes[h])
    for s in range(2):
        copy_to(t_ref.at[0], landed.at[s], send.at[0], recv.at[s], z, w).wait_recv()
    piece[...] = landed[0] + landed[1]
    spot = x_ref.at[pl.ds(pl.multiple_of(96 * q, 32), 96), pl.ds(pl.multiple_of(128 * m, 128), 128)]
    keep = pltpu.make_async_copy(piece, spot, local_sem)
    keep.start()
    rounds = [
        copy_to(piece, spot, send.at[1 + k], recv.at[1 + k], z, 16 * x + 2 * ((y + k) % 8) + c)
        for k in (4, 3, 5, 2, 6, 1, 7)
    ]
    for r in rounds:
        r.start()
    keep.wait()
    for r in rounds:
        r.wait_recv()
    slab = x_ref.at[pl.ds(pl.multiple_of(384 * x, 128), 384), pl.ds(pl.multiple_of(256 * c, 128), 256)]
    slabs = [
        copy_to(slab, slab, send.at[8 + k], recv.at[8 + k], z, 16 * ((x + k) % 4) + 2 * y + c)
        for k in (2, 1, 3)
    ]
    for r in slabs:
        r.start()
    for r in slabs:
        r.wait_recv()
    half = x_ref.at[:, pl.ds(pl.multiple_of(256 * c, 128), 256)]
    last = copy_to(half, half, send.at[12], recv.at[12], z, 16 * x + 2 * y + (1 - c))
    last.start()
    last.wait()
    for r in rounds + slabs:
        r.wait_send()
    for h in range(2):
        either_wait_send(t_ref.at[h], landed.at[e], send.at[h], recv.at[e], z, w, *homes[h])


def gather_tokens(tokens):
    e = lax.axis_index("wid") % 2
    wide = jnp.pad(tokens, ((0, 0), (0, 64)))
    wide = jnp.where(e == 0, wide, jnp.roll(wide, 64, axis=1)).reshape(2, 96, 128)
    return pl.pallas_call(
        tokens_kernel,
        out_shape=jax.ShapeDtypeStruct((1536, 512), BF16),
        in_specs=[pl.BlockSpec(memory_space=pltpu.VMEM)],
        out_specs=pl.BlockSpec(memory_space=pltpu.VMEM),
        scratch_shapes=[
            pltpu.VMEM((2, 96, 128), BF16),
            pltpu.VMEM((96, 128), BF16),
            pltpu.SemaphoreType.DMA((13,)),
            pltpu.SemaphoreType.DMA((13,)),
            pltpu.SemaphoreType.DMA,
        ],
        compiler_params=pltpu.CompilerParams(
            collective_id=0, has_side_effects=True, vmem_limit_bytes=VMEM_BYTES
        ),
        name="gather_tokens",
    )(wide)


def silu(v):
    return v / (1.0 + jnp.exp(-v))


def hidden_kernel(x_ref, w_ref, out_ref, got, sent, acc, hid, send, recv, ag_send, ag_recv):
    z, w, _, _, _ = position()
    toward = ((z + 1) % 8, (z + 7) % 8)
    barrier = pltpu.get_barrier_semaphore()
    for n in toward:
        signal(barrier, n, w)
    pl.semaphore_wait(barrier, 2)

    def product(owner, g):
        return lax.dot_general(
            w_ref[owner],
            x_ref[pl.ds(pl.multiple_of(384 * g, 128), 384), :],
            (((1,), (1,)), ((), ())),
            preferred_element_type=F32,
        )

    def hop(d, s, g):
        return copy_to(
            sent.at[d, s, g], got.at[d, s, g], send.at[d, s, g], recv.at[d, s, g], toward[d], w
        )

    def pass_on(d, s, g, add):
        owner = (z + 4 - s) % 8 if d == 0 else (z + 4 + s) % 8
        value = product(owner, g)
        if add:
            hop(d, s - 1, g).wait_recv()
            value = value + got[d, s - 1, g].astype(F32)
        sent[d, s, g] = value.astype(BF16)
        hop(d, s, g).start()

    @pl.loop(0, 2)
    def _(g):
        pass_on(0, 0, g, False)
        pass_on(1, 0, g + 2, False)

    @pl.loop(0, 2)
    def _(g):
        pass_on(0, 1, g + 2, False)
        pass_on(1, 1, g, False)

    @pl.loop(0, 2)
    def _(g):
        pass_on(0, 1, g, True)
        pass_on(1, 1, g + 2, True)

    for s in (2, 3):

        @pl.loop(0, 4)
        def _(g):
            pass_on(0, s, (g + 2) % 4, True)
            pass_on(1, s, g, True)

    @pl.loop(0, 4)
    def _(g):
        acc[g] = product(z, g)

    @pl.loop(0, 4)
    def _(g):
        hop(0, 3, g).wait_recv()
        hop(1, 3, g).wait_recv()
        total = acc[g] + got[0, 3, g].astype(F32) + got[1, 3, g].astype(F32)
        gate_a, up_a, gate_b, up_b = (total[32 * i : 32 * i + 32] for i in range(4))
        hid[0, g] = silu(gate_a) * up_a
        hid[1, g] = silu(gate_b) * up_b
        hid[2, g] = silu(0.5 * (gate_a + gate_b)) * (0.5 * (up_a + up_b))

    def stats(i):
        center = sum(jnp.sum(hid[i, g], axis=1, keepdims=True) for g in range(GROUPS)) / 1536.0
        spread = (
            sum(jnp.sum((hid[i, g] - center) ** 2, axis=1, keepdims=True) for g in range(GROUPS)) / 1536.0
        )
        return center, jnp.sqrt(spread + 1e-05)

    center_a, dev_a = stats(0)
    center_b, dev_b = stats(1)
    center_m, dev_m = stats(2)
    target_std = 0.5 * (dev_a + dev_b)
    target_mean = 0.5 * (center_a + center_b)
    for g in range(GROUPS):
        repaired = (hid[2, g] - center_m) / dev_m * target_std + target_mean
        out_ref[z, :, 384 * g : 384 * g + 384] = repaired.astype(BF16)

    def lap(d, s, h):
        slot = (z + 8 - s) % 8 if d == 0 else (z + s) % 8
        spot = out_ref.at[slot, :, pl.ds(768 * h, 768)]
        return copy_to(spot, spot, ag_send.at[d, s, h], ag_recv.at[d, s, h], toward[d], w)

    def arrived(d, s, h):
        slot = (z + 7 - s) % 8 if d == 0 else (z + 1 + s) % 8
        spot = out_ref.at[slot, :, pl.ds(768 * h, 768)]
        copy_to(spot, spot, ag_send.at[d, s, h], ag_recv.at[d, s, h], toward[d], w).wait_recv()

    laps = []
    for s in range(4):
        for i in range(2):
            for d in range(2):
                h = i if d == 0 else 1 - i
                if s == 3 and i == 1:
                    continue
                if s > 0:
                    arrived(d, s - 1, h)
                one = lap(d, s, h)
                one.start()
                laps.append(one)
    for d in range(2):
        arrived(d, 3, d)
        arrived(d, 2, 1 - d)
    for one in laps:
        one.wait_send()

    @pl.loop(0, 2)
    def _(g):
        hop(0, 0, g).wait_send()
        hop(1, 0, g + 2).wait_send()

    for s in (1, 2, 3):

        @pl.loop(0, 4)
        def _(g):
            hop(0, s, g).wait_send()
            hop(1, s, g).wait_send()


def hidden(x, weights):
    return pl.pallas_call(
        hidden_kernel,
        out_shape=jax.ShapeDtypeStruct((8, 32, 1536), BF16),
        in_specs=[pl.BlockSpec(memory_space=pltpu.VMEM)] * 2,
        out_specs=pl.BlockSpec(memory_space=pltpu.VMEM),
        scratch_shapes=[
            pltpu.VMEM((2, 4, GROUPS, 128, 384), BF16),
            pltpu.VMEM((2, 4, GROUPS, 128, 384), BF16),
            pltpu.VMEM((GROUPS, 128, 384), F32),
            pltpu.VMEM((3, GROUPS, 32, 384), F32),
            pltpu.SemaphoreType.DMA((2, 4, GROUPS)),
            pltpu.SemaphoreType.DMA((2, 4, GROUPS)),
            pltpu.SemaphoreType.DMA((2, 4, 2)),
            pltpu.SemaphoreType.DMA((2, 4, 2)),
        ],
        compiler_params=pltpu.CompilerParams(
            collective_id=1, has_side_effects=True, vmem_limit_bytes=VMEM_BYTES
        ),
        name="hidden",
    )(x, weights)


def merge_kernel(
    own_ref, other_ref, out_ref, c_got, x_sent, x_got, y_own, y_sent, y_got, final, send, recv
):
    z, w, x, y, c = position()
    q, m = piece_of(x, y, c)
    h = q % 2
    barrier = pltpu.get_barrier_semaphore()
    homes = [piece_home(z, w, i) for i in range(2)]
    targets = [(q // 2, 8 * z + 2 * m + s) for s in range(2)]
    greet(barrier, z, w, x, y, c, homes)
    order = (2, 1, 3, 0)
    swaps = []
    for k in order:
        at = (x + k) % 4
        swap = copy_to(
            other_ref.at[at], c_got.at[at], send.at[k], recv.at[k], z, 16 * x + 2 * y + (1 - c)
        )
        swap.start()
        swaps.append(swap)
    moves = []
    for swap, k in zip(swaps[:3], order[:3]):
        at = (x + k) % 4
        swap.wait_recv()
        x_sent[k - 1] = (own_ref[at] + c_got[at].astype(F32)).astype(BF16)
        move = copy_to(
            x_sent.at[k - 1], x_got.at[k - 1], send.at[3 + k], recv.at[3 + k], z, 16 * at + 2 * y + c
        )
        move.start()
        moves.append(move)
    swaps[3].wait_recv()
    for move in moves:
        move.wait_recv()
    for r in range(4):
        for l in range(2):
            rows, lanes = slice(96 * r, 96 * r + 96), slice(128 * l, 128 * l + 128)
            part = own_ref[x, rows, lanes] + c_got[x, rows, lanes].astype(F32)
            for k in range(3):
                part = part + x_got[k, rows, lanes].astype(F32)
            y_own[2 * r + l] = part
            y_sent[2 * r + l] = part.astype(BF16)
    for k in (4, 3, 5, 2, 6, 1, 7):
        at = (y + k) % 8
        move = copy_to(
            y_sent.at[at], y_got.at[k - 1], send.at[6 + k], recv.at[6 + k], z, 16 * x + 2 * at + c
        )
        move.start()
        moves.append(move)
    for move in moves[3:]:
        move.wait_recv()
    part = y_own[y]
    for k in range(7):
        part = part + y_got[k].astype(F32)
    final[...] = part.astype(BF16)
    for s in range(2):
        either_start(final, out_ref.at[h], send.at[14 + s], recv.at[14 + h], z, w, *targets[s])
    for i in range(2):
        copy_to(final, out_ref.at[i], send.at[14], recv.at[14 + i], z, w).wait_recv()
    for s in range(2):
        either_wait_send(final, out_ref.at[h], send.at[14 + s], recv.at[14 + h], z, w, *targets[s])
    for move in swaps + moves:
        move.wait_send()


def merge(own, other):
    return pl.pallas_call(
        merge_kernel,
        out_shape=jax.ShapeDtypeStruct((2, 96, 128), BF16),
        in_specs=[pl.BlockSpec(memory_space=pltpu.VMEM)] * 2,
        out_specs=pl.BlockSpec(memory_space=pltpu.VMEM),
        scratch_shapes=[
            pltpu.VMEM((4, 384, 256), BF16),
            pltpu.VMEM((3, 384, 256), BF16),
            pltpu.VMEM((3, 384, 256), BF16),
            pltpu.VMEM((8, 96, 128), F32),
            pltpu.VMEM((8, 96, 128), BF16),
            pltpu.VMEM((7, 96, 128), BF16),
            pltpu.VMEM((96, 128), BF16),
            pltpu.SemaphoreType.DMA((16,)),
            pltpu.SemaphoreType.DMA((16,)),
        ],
        compiler_params=pltpu.CompilerParams(
            collective_id=2, has_side_effects=True, vmem_limit_bytes=VMEM_BYTES
        ),
        name="merge",
    )(own, other)


def spread_rows(matrices):
    stacked = jnp.stack(matrices).reshape(6, 2, 64, 2, 512).transpose(2, 0, 1, 3, 4)
    dealt = lax.all_to_all(stacked, "wid", split_axis=0, concat_axis=0, tiled=True)
    return dealt.transpose(1, 0, 2, 3, 4).reshape(6, NB, 2, 512)


def local(tokens, gate_a, up_a, gate_b, up_b, down_a, down_b, block_perm):
    c = lax.axis_index("wid") % 2
    x = gather_tokens(tokens)
    rows = spread_rows((gate_a, up_a, gate_b, up_b, down_a, down_b))
    take = functools.partial(jnp.take, indices=block_perm, axis=0)
    weights = jnp.stack((rows[0], rows[1], take(rows[2]), take(rows[3])))
    weights = weights.reshape(4, 8, 32, 512).transpose(1, 0, 2, 3).reshape(8, 128, 512)
    down_mid = ((rows[4].astype(F32) + take(rows[5]).astype(F32)) * 0.5).astype(BF16).reshape(256, 512)
    repaired = hidden(x, weights).reshape(256, 1536)

    def share(which):
        part = lax.dynamic_slice_in_dim(down_mid, 256 * which, 256, 1)
        return lax.dot_general(
            repaired, part, (((0,), (0,)), ((), ())), preferred_element_type=F32
        ).reshape(4, 384, 256)

    merged = merge(share(c), share(1 - c).astype(BF16)).reshape(192, 128)
    return jnp.where(c == 0, merged[:, :64], merged[:, 64:])


def solution(mesh):
    return jax.shard_map(
        local,
        mesh=mesh,
        in_specs=(
            P("tok", "wid"),
            P("wid", "tok"),
            P("wid", "tok"),
            P("wid", "tok"),
            P("wid", "tok"),
            P("wid", "tok"),
            P("wid", "tok"),
            P(),
        ),
        out_specs=P("tok", "wid"),
        check_vma=False,
    )
```

```python
import functools

import jax
import jax.numpy as jnp
from jax import lax
from jax.experimental import pallas as pl
from jax.experimental.pallas import tpu as pltpu
from jax.sharding import PartitionSpec as P

NB = 128
GROUPS = 4
F32 = jnp.float32
BF16 = jnp.bfloat16
MESH_IDS = pl.DeviceIdType.MESH
VMEM_BYTES = 56 * 1024 * 1024


def copy_to(src, dst, send, recv, z, w):
    return pltpu.make_async_remote_copy(
        src_ref=src, dst_ref=dst, send_sem=send, recv_sem=recv, device_id=(z, w), device_id_type=MESH_IDS
    )


def signal(sem, z, w):
    pl.semaphore_signal(sem, inc=1, device_id=(z, w), device_id_type=MESH_IDS)


def position():
    z, w = lax.axis_index("tok"), lax.axis_index("wid")
    return z, w, w // 16, (w // 2) % 8, w % 2


def piece_of(x, y, c):
    return 4 * x + y // 2, 2 * c + y % 2


def piece_home(z, w, h):
    m = (w % 8) // 2
    return w // 8, 4 * (2 * z + h) + 2 * (m % 2) + m // 2


def greet(barrier, z, w, x, y, c, others):
    for k in range(1, 8):
        signal(barrier, z, 16 * x + 2 * ((y + k) % 8) + c)
    for k in range(1, 4):
        signal(barrier, z, 16 * ((x + k) % 4) + 2 * y + c)
    signal(barrier, z, 16 * x + 2 * y + (1 - c))
    own = 0
    for oz, ow in others:
        same = jnp.logical_and(oz == z, ow == w)
        own = own + same.astype(jnp.int32)

        @pl.when(jnp.logical_not(same))
        def _():
            signal(barrier, oz, ow)

    pl.semaphore_wait(barrier, 13 - own)


def either_start(src, dst, send, recv, z, w, oz, ow):
    same = jnp.logical_and(oz == z, ow == w)

    @pl.when(same)
    def _():
        pltpu.make_async_copy(src, dst, recv).start()

    @pl.when(jnp.logical_not(same))
    def _():
        copy_to(src, dst, send, recv, oz, ow).start()


def either_wait_send(src, dst, send, recv, z, w, oz, ow):
    same = jnp.logical_and(oz == z, ow == w)

    @pl.when(jnp.logical_not(same))
    def _():
        copy_to(src, dst, send, recv, oz, ow).wait_send()


def tokens_kernel(t_ref, x_ref, landed, piece, send, recv, local_sem):
    z, w, x, y, c = position()
    q, m = piece_of(x, y, c)
    e = w % 2
    barrier = pltpu.get_barrier_semaphore()
    sources = [(q // 2, 8 * z + 2 * m + s) for s in range(2)]
    homes = [piece_home(z, w, h) for h in range(2)]
    greet(barrier, z, w, x, y, c, sources)
    for h in range(2):
        either_start(t_ref.at[h], landed.at[e], send.at[h], recv.at[e], z, w, *homes[h])
    for s in range(2):
        copy_to(t_ref.at[0], landed.at[s], send.at[0], recv.at[s], z, w).wait_recv()
    piece[...] = landed[0] + landed[1]
    spot = x_ref.at[pl.ds(pl.multiple_of(96 * q, 32), 96), pl.ds(pl.multiple_of(128 * m, 128), 128)]
    keep = pltpu.make_async_copy(piece, spot, local_sem)
    keep.start()
    rounds = [
        copy_to(piece, spot, send.at[1 + k], recv.at[1 + k], z, 16 * x + 2 * ((y + k) % 8) + c)
        for k in (4, 3, 5, 2, 6, 1, 7)
    ]
    for r in rounds:
        r.start()
    keep.wait()
    for r in rounds:
        r.wait_recv()
    lanes = pl.ds(pl.multiple_of(256 * c, 128), 256)

    def slab(xs, start, size):
        return x_ref.at[pl.ds(pl.multiple_of(384 * xs + start, 64), size), lanes]

    def x_move(spot, i, d):
        to = (x + 1 + 2 * d) % 4
        return copy_to(spot, spot, send.at[9 + i], recv.at[9 + i], z, 16 * to + 2 * y + c)

    slabs = [x_move(slab(x, 192 * p, 192), 2 * d + p, d) for p, d in ((0, 0), (1, 1), (1, 0), (0, 1))]
    for r in slabs:
        r.start()
    for d in range(2):
        slabs[d].wait_recv()
        on = x_move(slab((x + 3 + 2 * d) % 4, 192 * d, 192), 4 + d, d)
        on.start()
        slabs.append(on)
    for r in slabs[2:]:
        r.wait_recv()
    half = x_ref.at[:, pl.ds(pl.multiple_of(256 * c, 128), 256)]
    last = copy_to(half, half, send.at[15], recv.at[15], z, 16 * x + 2 * y + (1 - c))
    last.start()
    last.wait()
    for r in rounds + slabs:
        r.wait_send()
    for h in range(2):
        either_wait_send(t_ref.at[h], landed.at[e], send.at[h], recv.at[e], z, w, *homes[h])


def gather_tokens(tokens):
    e = lax.axis_index("wid") % 2
    wide = jnp.pad(tokens, ((0, 0), (0, 64)))
    wide = jnp.where(e == 0, wide, jnp.roll(wide, 64, axis=1)).reshape(2, 96, 128)
    return pl.pallas_call(
        tokens_kernel,
        out_shape=jax.ShapeDtypeStruct((1536, 512), BF16),
        in_specs=[pl.BlockSpec(memory_space=pltpu.VMEM)],
        out_specs=pl.BlockSpec(memory_space=pltpu.VMEM),
        scratch_shapes=[
            pltpu.VMEM((2, 96, 128), BF16),
            pltpu.VMEM((96, 128), BF16),
            pltpu.SemaphoreType.DMA((16,)),
            pltpu.SemaphoreType.DMA((16,)),
            pltpu.SemaphoreType.DMA,
        ],
        compiler_params=pltpu.CompilerParams(
            collective_id=0, has_side_effects=True, vmem_limit_bytes=VMEM_BYTES
        ),
        name="gather_tokens",
    )(wide)


def silu(v):
    return v / (1.0 + jnp.exp(-v))


def ring_sum(x_ref, w_ref, got, sent, acc, send, recv, z, w, toward):
    def product(owner, g):
        return lax.dot_general(
            w_ref[owner],
            x_ref[pl.ds(pl.multiple_of(384 * g, 128), 384), :],
            (((1,), (1,)), ((), ())),
            preferred_element_type=F32,
        )

    def hop(d, s, g):
        return copy_to(
            sent.at[d, s, g], got.at[d, s, g], send.at[d, s, g], recv.at[d, s, g], toward[d], w
        )

    def pass_on(d, s, g, add):
        owner = (z + 4 - s) % 8 if d == 0 else (z + 4 + s) % 8
        value = product(owner, g)
        if add:
            hop(d, s - 1, g).wait_recv()
            value = value + got[d, s - 1, g].astype(F32)
        sent[d, s, g] = value.astype(BF16)
        hop(d, s, g).start()

    @pl.loop(0, 2)
    def _(g):
        pass_on(0, 0, g, False)
        pass_on(1, 0, g + 2, False)

    @pl.loop(0, 2)
    def _(g):
        pass_on(0, 1, g + 2, False)
        pass_on(1, 1, g, False)

    @pl.loop(0, 2)
    def _(g):
        pass_on(0, 1, g, True)
        pass_on(1, 1, g + 2, True)

    for s in (2, 3):

        @pl.loop(0, 4)
        def _(g):
            pass_on(0, s, (g + 2) % 4, True)
            pass_on(1, s, g, True)

    @pl.loop(0, 4)
    def _(g):
        acc[g] = product(z, g)

    @pl.loop(0, 4)
    def _(g):
        hop(0, 3, g).wait_recv()
        hop(1, 3, g).wait_recv()
        acc[g] = acc[g] + got[0, 3, g].astype(F32) + got[1, 3, g].astype(F32)

    def finish():
        @pl.loop(0, 2)
        def _(g):
            hop(0, 0, g).wait_send()
            hop(1, 0, g + 2).wait_send()

        for s in (1, 2, 3):

            @pl.loop(0, 4)
            def _(g):
                hop(0, s, g).wait_send()
                hop(1, s, g).wait_send()

    return finish


def ring_entry():
    z, w, _, _, _ = position()
    toward = ((z + 1) % 8, (z + 7) % 8)
    barrier = pltpu.get_barrier_semaphore()
    for n in toward:
        signal(barrier, n, w)
    pl.semaphore_wait(barrier, 2)
    return z, w, toward


RING_SCRATCH = [
    pltpu.VMEM((2, 4, GROUPS, 64, 384), BF16),
    pltpu.VMEM((2, 4, GROUPS, 64, 384), BF16),
    pltpu.SemaphoreType.DMA((2, 4, GROUPS)),
    pltpu.SemaphoreType.DMA((2, 4, GROUPS)),
]
RING_COST = pl.CostEstimate(flops=20_000_000_000, bytes_accessed=60_000_000, transcendentals=0)


def first_kernel(x_ref, w_ref, sum_ref, got, sent, send, recv):
    z, w, toward = ring_entry()
    ring_sum(x_ref, w_ref, got, sent, sum_ref, send, recv, z, w, toward)()


def first_sums(x, weights):
    return pl.pallas_call(
        first_kernel,
        out_shape=jax.ShapeDtypeStruct((GROUPS, 64, 384), F32),
        in_specs=[pl.BlockSpec(memory_space=pltpu.VMEM)] * 2,
        out_specs=pl.BlockSpec(memory_space=pltpu.VMEM),
        scratch_shapes=RING_SCRATCH,
        compiler_params=pltpu.CompilerParams(
            collective_id=3, has_side_effects=True, vmem_limit_bytes=VMEM_BYTES
        ),
        cost_estimate=RING_COST,
        name="first_sums",
    )(x, weights)


def hidden_kernel(x_ref, w_ref, a_ref, out_ref, got, sent, send, recv, acc, hid, ag_send, ag_recv):
    z, w, toward = ring_entry()
    finish = ring_sum(x_ref, w_ref, got, sent, acc, send, recv, z, w, toward)

    @pl.loop(0, 4)
    def _(g):
        gate_a, up_a = a_ref[g, :32], a_ref[g, 32:]
        gate_b, up_b = acc[g, :32], acc[g, 32:]
        hid[0, g] = silu(gate_a) * up_a
        hid[1, g] = silu(gate_b) * up_b
        hid[2, g] = silu(0.5 * (gate_a + gate_b)) * (0.5 * (up_a + up_b))

    def stats(i):
        center = sum(jnp.sum(hid[i, g], axis=1, keepdims=True) for g in range(GROUPS)) / 1536.0
        spread = (
            sum(jnp.sum((hid[i, g] - center) ** 2, axis=1, keepdims=True) for g in range(GROUPS)) / 1536.0
        )
        return center, jnp.sqrt(spread + 1e-05)

    center_a, dev_a = stats(0)
    center_b, dev_b = stats(1)
    center_m, dev_m = stats(2)
    target_std = 0.5 * (dev_a + dev_b)
    target_mean = 0.5 * (center_a + center_b)
    for g in range(GROUPS):
        repaired = (hid[2, g] - center_m) / dev_m * target_std + target_mean
        out_ref[z, :, 384 * g : 384 * g + 384] = repaired.astype(BF16)

    def lap(d, s, h):
        slot = (z + 8 - s) % 8 if d == 0 else (z + s) % 8
        spot = out_ref.at[slot, :, pl.ds(768 * h, 768)]
        return copy_to(spot, spot, ag_send.at[d, s, h], ag_recv.at[d, s, h], toward[d], w)

    def arrived(d, s, h):
        slot = (z + 7 - s) % 8 if d == 0 else (z + 1 + s) % 8
        spot = out_ref.at[slot, :, pl.ds(768 * h, 768)]
        copy_to(spot, spot, ag_send.at[d, s, h], ag_recv.at[d, s, h], toward[d], w).wait_recv()

    laps = []
    for s in range(4):
        for i in range(2):
            for d in range(2):
                h = i if d == 0 else 1 - i
                if s == 3 and i == 1:
                    continue
                if s > 0:
                    arrived(d, s - 1, h)
                one = lap(d, s, h)
                one.start()
                laps.append(one)
    for d in range(2):
        arrived(d, 3, d)
        arrived(d, 2, 1 - d)
    for one in laps:
        one.wait_send()
    finish()


def hidden(x, weights, sums_a):
    return pl.pallas_call(
        hidden_kernel,
        out_shape=jax.ShapeDtypeStruct((8, 32, 1536), BF16),
        in_specs=[pl.BlockSpec(memory_space=pltpu.VMEM)] * 3,
        out_specs=pl.BlockSpec(memory_space=pltpu.VMEM),
        scratch_shapes=RING_SCRATCH
        + [
            pltpu.VMEM((GROUPS, 64, 384), F32),
            pltpu.VMEM((3, GROUPS, 32, 384), F32),
            pltpu.SemaphoreType.DMA((2, 4, 2)),
            pltpu.SemaphoreType.DMA((2, 4, 2)),
        ],
        compiler_params=pltpu.CompilerParams(
            collective_id=1, has_side_effects=True, vmem_limit_bytes=VMEM_BYTES
        ),
        cost_estimate=RING_COST,
        name="hidden",
    )(x, weights, sums_a)


def merge_kernel(
    own_ref, other_ref, out_ref, c_got, far_sent, far_got, near_sent, near_got, y_own, y_got, final, send, recv
):
    z, w, x, y, c = position()
    q, m = piece_of(x, y, c)
    h = q % 2
    barrier = pltpu.get_barrier_semaphore()
    homes = [piece_home(z, w, i) for i in range(2)]
    targets = [(q // 2, 8 * z + 2 * m + s) for s in range(2)]
    greet(barrier, z, w, x, y, c, homes)
    order = (2, 1, 3, 0)
    swaps = []
    for k in order:
        at = (x + k) % 4
        swap = copy_to(
            other_ref.at[at], c_got.at[at], send.at[k], recv.at[k], z, 16 * x + 2 * y + (1 - c)
        )
        swap.start()
        swaps.append(swap)

    def x_move(src, dst, i, d):
        to = (x + 1 + 2 * d) % 4
        return copy_to(src, dst, send.at[4 + i], recv.at[4 + i], z, 16 * to + 2 * y + c)

    moves = []
    swaps[0].wait_recv()
    at = (x + 2) % 4
    for d in range(2):
        rows = slice(192 * d, 192 * d + 192)
        far_sent[d] = (own_ref[at, rows] + c_got[at, rows]).astype(BF16)
        move = x_move(far_sent.at[d], far_got.at[d], d, d)
        move.start()
        moves.append(move)
    for d in range(2):
        at = (x + 1 + 2 * d) % 4
        swaps[1 + d].wait_recv()
        for part in (1 - d, d):
            rows = slice(192 * part, 192 * part + 192)
            value = own_ref[at, rows] + c_got[at, rows]
            if part == d:
                moves[d].wait_recv()
                value = value + far_got[d].astype(F32)
            near_sent[d, part] = value.astype(BF16)
            move = x_move(near_sent.at[d, part], near_got.at[d, part], 2 + 2 * d + part, d)
            move.start()
            moves.append(move)
    swaps[3].wait_recv()
    for move in moves[2:]:
        move.wait_recv()
    for r in range(4):
        for l in range(2):
            rows, lanes = slice(96 * r, 96 * r + 96), slice(128 * l, 128 * l + 128)
            inner = slice(96 * (r % 2), 96 * (r % 2) + 96)
            part = own_ref[x, rows, lanes] + c_got[x, rows, lanes]
            for d in range(2):
                part = part + near_got[d, r // 2, inner, lanes].astype(F32)
            y_own[2 * r + l] = part
    for k in (4, 3, 5, 2, 6, 1, 7):
        at = (y + k) % 8
        move = copy_to(
            y_own.at[at], y_got.at[k - 1], send.at[9 + k], recv.at[9 + k], z, 16 * x + 2 * at + c
        )
        move.start()
        moves.append(move)
    for move in moves[6:]:
        move.wait_recv()
    part = y_own[y]
    for k in range(7):
        part = part + y_got[k]
    final[...] = part.astype(BF16)
    for s in range(2):
        either_start(final, out_ref.at[h], send.at[17 + s], recv.at[17 + h], z, w, *targets[s])
    for i in range(2):
        copy_to(final, out_ref.at[i], send.at[17], recv.at[17 + i], z, w).wait_recv()
    for s in range(2):
        either_wait_send(final, out_ref.at[h], send.at[17 + s], recv.at[17 + h], z, w, *targets[s])
    for move in swaps + moves:
        move.wait_send()


def merge(own, other):
    return pl.pallas_call(
        merge_kernel,
        out_shape=jax.ShapeDtypeStruct((2, 96, 128), BF16),
        in_specs=[pl.BlockSpec(memory_space=pltpu.VMEM)] * 2,
        out_specs=pl.BlockSpec(memory_space=pltpu.VMEM),
        scratch_shapes=[
            pltpu.VMEM((4, 384, 256), F32),
            pltpu.VMEM((2, 192, 256), BF16),
            pltpu.VMEM((2, 192, 256), BF16),
            pltpu.VMEM((2, 2, 192, 256), BF16),
            pltpu.VMEM((2, 2, 192, 256), BF16),
            pltpu.VMEM((8, 96, 128), F32),
            pltpu.VMEM((7, 96, 128), F32),
            pltpu.VMEM((96, 128), BF16),
            pltpu.SemaphoreType.DMA((19,)),
            pltpu.SemaphoreType.DMA((19,)),
        ],
        compiler_params=pltpu.CompilerParams(
            collective_id=2, has_side_effects=True, vmem_limit_bytes=VMEM_BYTES
        ),
        name="merge",
    )(own, other)


def spread_rows(*matrices):
    stacked = jnp.stack(matrices).reshape(2, 2, 64, 2, 512).transpose(2, 0, 1, 3, 4)
    dealt = lax.all_to_all(stacked, "wid", split_axis=0, concat_axis=0, tiled=True)
    return dealt.transpose(1, 0, 2, 3, 4).reshape(2, NB, 2, 512)


def by_owner(gate, up):
    both = jnp.stack((gate, up)).reshape(2, 8, 32, 512)
    return both.transpose(1, 0, 2, 3).reshape(8, 64, 512)


def local(tokens, gate_a, up_a, gate_b, up_b, down_a, down_b, block_perm):
    c = lax.axis_index("wid") % 2
    take = functools.partial(jnp.take, indices=block_perm, axis=0)
    rows_a = spread_rows(gate_a, up_a)
    x = gather_tokens(tokens)
    gate_b, up_b, rows_a = lax.optimization_barrier((gate_b, up_b, rows_a))
    rows_b = spread_rows(gate_b, up_b)
    sums_a = first_sums(x, by_owner(rows_a[0], rows_a[1]))
    down_a, down_b, rows_b = lax.optimization_barrier((down_a, down_b, rows_b))
    rows_d = spread_rows(down_a, down_b)
    repaired = hidden(x, by_owner(take(rows_b[0]), take(rows_b[1])), sums_a).reshape(256, 1536)
    down_mid = ((rows_d[0].astype(F32) + take(rows_d[1]).astype(F32)) * 0.5).astype(BF16).reshape(256, 512)

    def share(which):
        part = lax.dynamic_slice_in_dim(down_mid, 256 * which, 256, 1)
        return lax.dot_general(
            repaired, part, (((0,), (0,)), ((), ())), preferred_element_type=F32
        ).reshape(4, 384, 256)

    merged = merge(share(c), share(1 - c)).reshape(192, 128)
    return jnp.where(c == 0, merged[:, :64], merged[:, 64:])


def solution(mesh):
    return jax.shard_map(
        local,
        mesh=mesh,
        in_specs=(
            P("tok", "wid"),
            P("wid", "tok"),
            P("wid", "tok"),
            P("wid", "tok"),
            P("wid", "tok"),
            P("wid", "tok"),
            P("wid", "tok"),
            P(),
        ),
        out_specs=P("tok", "wid"),
        check_vma=False,
    )
```

```python
import functools

import jax
import jax.numpy as jnp
from jax import lax
from jax.experimental import pallas as pl
from jax.experimental.pallas import tpu as pltpu
from jax.sharding import PartitionSpec as P

NB = 128
GROUPS = 4
F32 = jnp.float32
BF16 = jnp.bfloat16
MESH_IDS = pl.DeviceIdType.MESH
VMEM_BYTES = 56 * 1024 * 1024


def copy_to(src, dst, send, recv, z, w):
    return pltpu.make_async_remote_copy(
        src_ref=src, dst_ref=dst, send_sem=send, recv_sem=recv, device_id=(z, w), device_id_type=MESH_IDS
    )


def signal(sem, z, w):
    pl.semaphore_signal(sem, inc=1, device_id=(z, w), device_id_type=MESH_IDS)


def position():
    z, w = lax.axis_index("tok"), lax.axis_index("wid")
    return z, w, w // 16, (w // 2) % 8, w % 2


def piece_of(x, y, c):
    return 4 * x + y // 2, 2 * c + y % 2


def piece_home(z, w, h):
    m = (w % 8) // 2
    return w // 8, 4 * (2 * z + h) + 2 * (m % 2) + m // 2


def greet(barrier, z, w, x, y, c, others):
    for k in range(1, 8):
        signal(barrier, z, 16 * x + 2 * ((y + k) % 8) + c)
    for k in range(1, 4):
        signal(barrier, z, 16 * ((x + k) % 4) + 2 * y + c)
    signal(barrier, z, 16 * x + 2 * y + (1 - c))
    greet_others(barrier, z, w, others, 11)


def greet_others(barrier, z, w, others, already):
    own = 0
    for oz, ow in others:
        same = jnp.logical_and(oz == z, ow == w)
        own = own + same.astype(jnp.int32)

        @pl.when(jnp.logical_not(same))
        def _():
            signal(barrier, oz, ow)

    pl.semaphore_wait(barrier, already + len(others) - own)


def either_start(src, dst, send, recv, z, w, oz, ow):
    same = jnp.logical_and(oz == z, ow == w)

    @pl.when(same)
    def _():
        pltpu.make_async_copy(src, dst, recv).start()

    @pl.when(jnp.logical_not(same))
    def _():
        copy_to(src, dst, send, recv, oz, ow).start()


def either_wait_send(src, dst, send, recv, z, w, oz, ow):
    same = jnp.logical_and(oz == z, ow == w)

    @pl.when(jnp.logical_not(same))
    def _():
        copy_to(src, dst, send, recv, oz, ow).wait_send()


def deal(src, dst, send, recv, z, w, low, high, act):
    @pl.loop(low, high)
    def _(k):
        to = (w + k) % 64
        act(copy_to(src.at[to], dst.at[w], send.at[k], recv.at[k], z, to))


def deal_start(src, dst, send, recv, z, w, low, high):
    deal(src, dst, send, recv, z, w, low, high, lambda one: one.start())


def deal_wait(src, dst, send, recv, z, w):
    pltpu.make_async_copy(src.at[w], dst.at[w], recv.at[0]).wait()
    deal(src, dst, send, recv, z, w, 1, 64, lambda one: one.wait())


def greet_plane(barrier, z, w):
    @pl.loop(1, 64)
    def _(k):
        signal(barrier, z, (w + k) % 64)


def tokens_kernel(t_ref, r_ref, x_ref, dealt, landed, piece, send, recv, local_sem, d_send, d_recv):
    z, w, x, y, c = position()
    q, m = piece_of(x, y, c)
    e = w % 2
    barrier = pltpu.get_barrier_semaphore()
    sources = [(q // 2, 8 * z + 2 * m + s) for s in range(2)]
    homes = [piece_home(z, w, h) for h in range(2)]
    greet_plane(barrier, z, w)
    greet_others(barrier, z, w, sources, 63)
    for h in range(2):
        either_start(t_ref.at[h], landed.at[e], send.at[h], recv.at[e], z, w, *homes[h])
    for s in range(2):
        copy_to(t_ref.at[0], landed.at[s], send.at[0], recv.at[s], z, w).wait_recv()
    piece[...] = landed[0] + landed[1]
    spot = x_ref.at[pl.ds(pl.multiple_of(96 * q, 32), 96), pl.ds(pl.multiple_of(128 * m, 128), 128)]
    keep = pltpu.make_async_copy(piece, spot, local_sem)
    keep.start()
    rounds = [
        copy_to(piece, spot, send.at[1 + k], recv.at[1 + k], z, 16 * x + 2 * ((y + k) % 8) + c)
        for k in (4, 3, 5, 2, 6, 1, 7)
    ]
    for r in rounds:
        r.start()
    pltpu.make_async_copy(r_ref.at[w], dealt.at[w], d_recv.at[0]).start()
    deal_start(r_ref, dealt, d_send, d_recv, z, w, 1, 24)
    keep.wait()
    for r in rounds:
        r.wait_recv()
    lanes = pl.ds(pl.multiple_of(256 * c, 128), 256)

    def slab(xs, start, size):
        return x_ref.at[pl.ds(pl.multiple_of(384 * xs + start, 64), size), lanes]

    def x_move(spot, i, d):
        to = (x + 1 + 2 * d) % 4
        return copy_to(spot, spot, send.at[9 + i], recv.at[9 + i], z, 16 * to + 2 * y + c)

    slabs = [x_move(slab(x, 192 * p, 192), 2 * d + p, d) for p, d in ((0, 0), (1, 1), (1, 0), (0, 1))]
    for r in slabs:
        r.start()
    deal_start(r_ref, dealt, d_send, d_recv, z, w, 24, 44)
    for d in range(2):
        slabs[d].wait_recv()
        on = x_move(slab((x + 3 + 2 * d) % 4, 192 * d, 192), 4 + d, d)
        on.start()
        slabs.append(on)
    deal_start(r_ref, dealt, d_send, d_recv, z, w, 44, 64)
    for r in slabs[2:]:
        r.wait_recv()
    half = x_ref.at[:, pl.ds(pl.multiple_of(256 * c, 128), 256)]
    last = copy_to(half, half, send.at[15], recv.at[15], z, 16 * x + 2 * y + (1 - c))
    last.start()
    last.wait()
    for r in rounds + slabs:
        r.wait_send()
    deal_wait(r_ref, dealt, d_send, d_recv, z, w)
    for h in range(2):
        either_wait_send(t_ref.at[h], landed.at[e], send.at[h], recv.at[e], z, w, *homes[h])


def gather_tokens(tokens, rows):
    e = lax.axis_index("wid") % 2
    wide = jnp.pad(tokens, ((0, 0), (0, 64)))
    wide = jnp.where(e == 0, wide, jnp.roll(wide, 64, axis=1)).reshape(2, 96, 128)
    return pl.pallas_call(
        tokens_kernel,
        out_shape=(jax.ShapeDtypeStruct((1536, 512), BF16), jax.ShapeDtypeStruct(rows.shape, BF16)),
        in_specs=[pl.BlockSpec(memory_space=pltpu.VMEM)] * 2,
        out_specs=[pl.BlockSpec(memory_space=pltpu.VMEM)] * 2,
        scratch_shapes=[
            pltpu.VMEM((2, 96, 128), BF16),
            pltpu.VMEM((96, 128), BF16),
            pltpu.SemaphoreType.DMA((16,)),
            pltpu.SemaphoreType.DMA((16,)),
            pltpu.SemaphoreType.DMA,
            pltpu.SemaphoreType.DMA((64,)),
            pltpu.SemaphoreType.DMA((64,)),
        ],
        compiler_params=pltpu.CompilerParams(
            collective_id=0, has_side_effects=True, vmem_limit_bytes=VMEM_BYTES
        ),
        name="gather_tokens",
    )(wide, rows)


def silu(v):
    return v / (1.0 + jnp.exp(-v))


def ring_sum(x_ref, w_ref, got, sent, acc, send, recv, z, w, toward):
    def product(owner, g):
        return lax.dot_general(
            w_ref[owner],
            x_ref[pl.ds(pl.multiple_of(384 * g, 128), 384), :],
            (((1,), (1,)), ((), ())),
            preferred_element_type=F32,
        )

    def hop(d, s, g):
        return copy_to(
            sent.at[d, s, g], got.at[d, s, g], send.at[d, s, g], recv.at[d, s, g], toward[d], w
        )

    def pass_on(d, s, g, add):
        owner = (z + 4 - s) % 8 if d == 0 else (z + 4 + s) % 8
        value = product(owner, g)
        if add:
            hop(d, s - 1, g).wait_recv()
            value = value + got[d, s - 1, g].astype(F32)
        sent[d, s, g] = value.astype(BF16)
        hop(d, s, g).start()

    @pl.loop(0, 2)
    def _(g):
        pass_on(0, 0, g, False)
        pass_on(1, 0, g + 2, False)

    @pl.loop(0, 2)
    def _(g):
        pass_on(0, 1, g + 2, False)
        pass_on(1, 1, g, False)

    @pl.loop(0, 2)
    def _(g):
        pass_on(0, 1, g, True)
        pass_on(1, 1, g + 2, True)

    for s in (2, 3):

        @pl.loop(0, 4)
        def _(g):
            pass_on(0, s, (g + 2) % 4, True)
            pass_on(1, s, g, True)

    @pl.loop(0, 4)
    def _(g):
        acc[g] = product(z, g)

    @pl.loop(0, 4)
    def _(g):
        hop(0, 3, g).wait_recv()
        hop(1, 3, g).wait_recv()
        acc[g] = acc[g] + got[0, 3, g].astype(F32) + got[1, 3, g].astype(F32)

    def finish():
        @pl.loop(0, 2)
        def _(g):
            hop(0, 0, g).wait_send()
            hop(1, 0, g + 2).wait_send()

        for s in (1, 2, 3):

            @pl.loop(0, 4)
            def _(g):
                hop(0, s, g).wait_send()
                hop(1, s, g).wait_send()

    return finish


RING_SCRATCH = [
    pltpu.VMEM((2, 4, GROUPS, 128, 384), BF16),
    pltpu.VMEM((2, 4, GROUPS, 128, 384), BF16),
    pltpu.SemaphoreType.DMA((2, 4, GROUPS)),
    pltpu.SemaphoreType.DMA((2, 4, GROUPS)),
]


def hidden_kernel(
    x_ref, w_ref, r_ref, out_ref, dealt, got, sent, send, recv, acc, hid, ag_send, ag_recv, d_send, d_recv
):
    z, w, _, _, _ = position()
    toward = ((z + 1) % 8, (z + 7) % 8)
    barrier = pltpu.get_barrier_semaphore()
    for n in toward:
        signal(barrier, n, w)
    greet_plane(barrier, z, w)
    pl.semaphore_wait(barrier, 65)
    pltpu.make_async_copy(r_ref.at[w], dealt.at[w], d_recv.at[0]).start()
    deal_start(r_ref, dealt, d_send, d_recv, z, w, 1, 64)
    finish = ring_sum(x_ref, w_ref, got, sent, acc, send, recv, z, w, toward)

    @pl.loop(0, 4)
    def _(g):
        gate_a, up_a, gate_b, up_b = (acc[g, 32 * i : 32 * i + 32] for i in range(4))
        hid[0, g] = silu(gate_a) * up_a
        hid[1, g] = silu(gate_b) * up_b
        hid[2, g] = silu(0.5 * (gate_a + gate_b)) * (0.5 * (up_a + up_b))

    def stats(i):
        center = sum(jnp.sum(hid[i, g], axis=1, keepdims=True) for g in range(GROUPS)) / 1536.0
        spread = (
            sum(jnp.sum((hid[i, g] - center) ** 2, axis=1, keepdims=True) for g in range(GROUPS)) / 1536.0
        )
        return center, jnp.sqrt(spread + 1e-05)

    center_a, dev_a = stats(0)
    center_b, dev_b = stats(1)
    center_m, dev_m = stats(2)
    target_std = 0.5 * (dev_a + dev_b)
    target_mean = 0.5 * (center_a + center_b)
    for g in range(GROUPS):
        repaired = (hid[2, g] - center_m) / dev_m * target_std + target_mean
        out_ref[z, :, 384 * g : 384 * g + 384] = repaired.astype(BF16)

    def lap(d, s, h):
        slot = (z + 8 - s) % 8 if d == 0 else (z + s) % 8
        spot = out_ref.at[slot, :, pl.ds(768 * h, 768)]
        return copy_to(spot, spot, ag_send.at[d, s, h], ag_recv.at[d, s, h], toward[d], w)

    def arrived(d, s, h):
        slot = (z + 7 - s) % 8 if d == 0 else (z + 1 + s) % 8
        spot = out_ref.at[slot, :, pl.ds(768 * h, 768)]
        copy_to(spot, spot, ag_send.at[d, s, h], ag_recv.at[d, s, h], toward[d], w).wait_recv()

    laps = []
    for s in range(4):
        for i in range(2):
            for d in range(2):
                h = i if d == 0 else 1 - i
                if s == 3 and i == 1:
                    continue
                if s > 0:
                    arrived(d, s - 1, h)
                one = lap(d, s, h)
                one.start()
                laps.append(one)
    for d in range(2):
        arrived(d, 3, d)
        arrived(d, 2, 1 - d)
    for one in laps:
        one.wait_send()
    finish()
    deal_wait(r_ref, dealt, d_send, d_recv, z, w)


def hidden(x, weights, rows):
    return pl.pallas_call(
        hidden_kernel,
        out_shape=(jax.ShapeDtypeStruct((8, 32, 1536), BF16), jax.ShapeDtypeStruct(rows.shape, BF16)),
        in_specs=[pl.BlockSpec(memory_space=pltpu.VMEM)] * 3,
        out_specs=[pl.BlockSpec(memory_space=pltpu.VMEM)] * 2,
        scratch_shapes=RING_SCRATCH
        + [
            pltpu.VMEM((GROUPS, 128, 384), F32),
            pltpu.VMEM((3, GROUPS, 32, 384), F32),
            pltpu.SemaphoreType.DMA((2, 4, 2)),
            pltpu.SemaphoreType.DMA((2, 4, 2)),
            pltpu.SemaphoreType.DMA((64,)),
            pltpu.SemaphoreType.DMA((64,)),
        ],
        compiler_params=pltpu.CompilerParams(
            collective_id=1, has_side_effects=True, vmem_limit_bytes=VMEM_BYTES
        ),
        name="hidden",
    )(x, weights, rows)


def merge_kernel(
    own_ref, other_ref, out_ref, c_got, far_sent, far_got, near_sent, near_got, y_own, y_got, final, send, recv
):
    z, w, x, y, c = position()
    q, m = piece_of(x, y, c)
    h = q % 2
    barrier = pltpu.get_barrier_semaphore()
    homes = [piece_home(z, w, i) for i in range(2)]
    targets = [(q // 2, 8 * z + 2 * m + s) for s in range(2)]
    greet(barrier, z, w, x, y, c, homes)
    order = (2, 1, 3, 0)
    swaps = []
    for k in order:
        at = (x + k) % 4
        swap = copy_to(
            other_ref.at[at], c_got.at[at], send.at[k], recv.at[k], z, 16 * x + 2 * y + (1 - c)
        )
        swap.start()
        swaps.append(swap)

    def x_move(src, dst, i, d):
        to = (x + 1 + 2 * d) % 4
        return copy_to(src, dst, send.at[4 + i], recv.at[4 + i], z, 16 * to + 2 * y + c)

    moves = []
    swaps[0].wait_recv()
    at = (x + 2) % 4
    for d in range(2):
        rows = slice(192 * d, 192 * d + 192)
        far_sent[d] = (own_ref[at, rows] + c_got[at, rows]).astype(BF16)
        move = x_move(far_sent.at[d], far_got.at[d], d, d)
        move.start()
        moves.append(move)
    for d in range(2):
        at = (x + 1 + 2 * d) % 4
        swaps[1 + d].wait_recv()
        for part in (1 - d, d):
            rows = slice(192 * part, 192 * part + 192)
            value = own_ref[at, rows] + c_got[at, rows]
            if part == d:
                moves[d].wait_recv()
                value = value + far_got[d].astype(F32)
            near_sent[d, part] = value.astype(BF16)
            move = x_move(near_sent.at[d, part], near_got.at[d, part], 2 + 2 * d + part, d)
            move.start()
            moves.append(move)
    swaps[3].wait_recv()
    for move in moves[2:]:
        move.wait_recv()
    for r in range(4):
        for l in range(2):
            rows, lanes = slice(96 * r, 96 * r + 96), slice(128 * l, 128 * l + 128)
            inner = slice(96 * (r % 2), 96 * (r % 2) + 96)
            part = own_ref[x, rows, lanes] + c_got[x, rows, lanes]
            for d in range(2):
                part = part + near_got[d, r // 2, inner, lanes].astype(F32)
            y_own[2 * r + l] = part
    for k in (4, 3, 5, 2, 6, 1, 7):
        at = (y + k) % 8
        move = copy_to(
            y_own.at[at], y_got.at[k - 1], send.at[9 + k], recv.at[9 + k], z, 16 * x + 2 * at + c
        )
        move.start()
        moves.append(move)
    for move in moves[6:]:
        move.wait_recv()
    part = y_own[y]
    for k in range(7):
        part = part + y_got[k]
    final[...] = part.astype(BF16)
    for s in range(2):
        either_start(final, out_ref.at[h], send.at[17 + s], recv.at[17 + h], z, w, *targets[s])
    for i in range(2):
        copy_to(final, out_ref.at[i], send.at[17], recv.at[17 + i], z, w).wait_recv()
    for s in range(2):
        either_wait_send(final, out_ref.at[h], send.at[17 + s], recv.at[17 + h], z, w, *targets[s])
    for move in swaps + moves:
        move.wait_send()


def merge(own, other):
    return pl.pallas_call(
        merge_kernel,
        out_shape=jax.ShapeDtypeStruct((2, 96, 128), BF16),
        in_specs=[pl.BlockSpec(memory_space=pltpu.VMEM)] * 2,
        out_specs=pl.BlockSpec(memory_space=pltpu.VMEM),
        scratch_shapes=[
            pltpu.VMEM((4, 384, 256), F32),
            pltpu.VMEM((2, 192, 256), BF16),
            pltpu.VMEM((2, 192, 256), BF16),
            pltpu.VMEM((2, 2, 192, 256), BF16),
            pltpu.VMEM((2, 2, 192, 256), BF16),
            pltpu.VMEM((8, 96, 128), F32),
            pltpu.VMEM((7, 96, 128), F32),
            pltpu.VMEM((96, 128), BF16),
            pltpu.SemaphoreType.DMA((19,)),
            pltpu.SemaphoreType.DMA((19,)),
        ],
        compiler_params=pltpu.CompilerParams(
            collective_id=2, has_side_effects=True, vmem_limit_bytes=VMEM_BYTES
        ),
        name="merge",
    )(own, other)


def by_dest(*matrices):
    n = len(matrices)
    return jnp.stack(matrices).reshape(n, 2, 64, 2, 512).transpose(2, 0, 1, 3, 4)


def by_block(dealt):
    n = dealt.shape[1]
    return dealt.transpose(1, 0, 2, 3, 4).reshape(n, NB, 2, 512)


def local(tokens, gate_a, up_a, gate_b, up_b, down_a, down_b, block_perm):
    c = lax.axis_index("wid") % 2
    take = functools.partial(jnp.take, indices=block_perm, axis=0)
    x, rows = gather_tokens(tokens, by_dest(gate_a, up_a, gate_b, up_b))
    rows = by_block(rows)
    weights = jnp.stack((rows[0], rows[1], take(rows[2]), take(rows[3])))
    weights = weights.reshape(4, 8, 32, 512).transpose(1, 0, 2, 3).reshape(8, 128, 512)
    repaired, rows = hidden(x, weights, by_dest(down_a, down_b))
    repaired = repaired.reshape(256, 1536)
    rows = by_block(rows)
    down_mid = ((rows[0].astype(F32) + take(rows[1]).astype(F32)) * 0.5).astype(BF16).reshape(256, 512)

    def share(which):
        part = lax.dynamic_slice_in_dim(down_mid, 256 * which, 256, 1)
        return lax.dot_general(
            repaired, part, (((0,), (0,)), ((), ())), preferred_element_type=F32
        ).reshape(4, 384, 256)

    merged = merge(share(c), share(1 - c)).reshape(192, 128)
    return jnp.where(c == 0, merged[:, :64], merged[:, 64:])


def solution(mesh):
    return jax.shard_map(
        local,
        mesh=mesh,
        in_specs=(
            P("tok", "wid"),
            P("wid", "tok"),
            P("wid", "tok"),
            P("wid", "tok"),
            P("wid", "tok"),
            P("wid", "tok"),
            P("wid", "tok"),
            P(),
        ),
        out_specs=P("tok", "wid"),
        check_vma=False,
    )
```

```python
import functools

import jax
import jax.numpy as jnp
from jax import lax
from jax.experimental import pallas as pl
from jax.experimental.pallas import tpu as pltpu
from jax.sharding import PartitionSpec as P

NB = 128
GROUPS = 4
F32 = jnp.float32
BF16 = jnp.bfloat16
MESH_IDS = pl.DeviceIdType.MESH
VMEM_BYTES = 56 * 1024 * 1024


def copy_to(src, dst, send, recv, z, w):
    return pltpu.make_async_remote_copy(
        src_ref=src, dst_ref=dst, send_sem=send, recv_sem=recv, device_id=(z, w), device_id_type=MESH_IDS
    )


def signal(sem, z, w):
    pl.semaphore_signal(sem, inc=1, device_id=(z, w), device_id_type=MESH_IDS)


def position():
    z, w = lax.axis_index("tok"), lax.axis_index("wid")
    return z, w, w // 16, (w // 2) % 8, w % 2


def piece_of(x, y, c):
    return 4 * x + y // 2, 2 * c + y % 2


def piece_home(z, w, h):
    m = (w % 8) // 2
    return w // 8, 4 * (2 * z + h) + 2 * (m % 2) + m // 2


def greet(barrier, z, w, x, y, c, others):
    for k in range(1, 8):
        signal(barrier, z, 16 * x + 2 * ((y + k) % 8) + c)
    for k in range(1, 4):
        signal(barrier, z, 16 * ((x + k) % 4) + 2 * y + c)
    signal(barrier, z, 16 * x + 2 * y + (1 - c))
    greet_others(barrier, z, w, others, 11)


def greet_others(barrier, z, w, others, already):
    own = 0
    for oz, ow in others:
        same = jnp.logical_and(oz == z, ow == w)
        own = own + same.astype(jnp.int32)

        @pl.when(jnp.logical_not(same))
        def _():
            signal(barrier, oz, ow)

    pl.semaphore_wait(barrier, already + len(others) - own)


def either_start(src, dst, send, recv, z, w, oz, ow):
    same = jnp.logical_and(oz == z, ow == w)

    @pl.when(same)
    def _():
        pltpu.make_async_copy(src, dst, recv).start()

    @pl.when(jnp.logical_not(same))
    def _():
        copy_to(src, dst, send, recv, oz, ow).start()


def either_wait_send(src, dst, send, recv, z, w, oz, ow):
    same = jnp.logical_and(oz == z, ow == w)

    @pl.when(jnp.logical_not(same))
    def _():
        copy_to(src, dst, send, recv, oz, ow).wait_send()


def deal(src, dst, send, recv, z, w, low, high, act):
    @pl.loop(low, high)
    def _(k):
        to = (w + k) % 64
        act(copy_to(src.at[to], dst.at[w], send.at[k], recv.at[k], z, to))


def deal_start(src, dst, send, recv, z, w, low, high):
    deal(src, dst, send, recv, z, w, low, high, lambda one: one.start())


def deal_wait(src, dst, send, recv, z, w):
    pltpu.make_async_copy(src.at[w], dst.at[w], recv.at[0]).wait()
    deal(src, dst, send, recv, z, w, 1, 64, lambda one: one.wait())


def greet_plane(barrier, z, w):
    @pl.loop(1, 64)
    def _(k):
        signal(barrier, z, (w + k) % 64)


def tokens_kernel(t_ref, r_ref, x_ref, dealt, landed, piece, send, recv, local_sem, d_send, d_recv):
    z, w, x, y, c = position()
    q, m = piece_of(x, y, c)
    e = w % 2
    barrier = pltpu.get_barrier_semaphore()
    sources = [(q // 2, 8 * z + 2 * m + s) for s in range(2)]
    homes = [piece_home(z, w, h) for h in range(2)]
    greet_plane(barrier, z, w)
    greet_others(barrier, z, w, sources, 63)
    for h in range(2):
        either_start(t_ref.at[h], landed.at[e], send.at[h], recv.at[e], z, w, *homes[h])
    pltpu.make_async_copy(r_ref.at[w], dealt.at[w], d_recv.at[0]).start()
    deal_start(r_ref, dealt, d_send, d_recv, z, w, 1, 12)
    for s in range(2):
        copy_to(t_ref.at[0], landed.at[s], send.at[0], recv.at[s], z, w).wait_recv()
    piece[...] = landed[0] + landed[1]
    spot = x_ref.at[pl.ds(pl.multiple_of(96 * q, 32), 96), pl.ds(pl.multiple_of(128 * m, 128), 128)]
    keep = pltpu.make_async_copy(piece, spot, local_sem)
    keep.start()
    rounds = [
        copy_to(piece, spot, send.at[1 + k], recv.at[1 + k], z, 16 * x + 2 * ((y + k) % 8) + c)
        for k in (4, 3, 5, 2, 6, 1, 7)
    ]
    for r in rounds:
        r.start()
    deal_start(r_ref, dealt, d_send, d_recv, z, w, 12, 28)
    keep.wait()
    for r in rounds:
        r.wait_recv()
    lanes = pl.ds(pl.multiple_of(256 * c, 128), 256)

    def slab(xs, start, size):
        return x_ref.at[pl.ds(pl.multiple_of(384 * xs + start, 64), size), lanes]

    def x_move(spot, i, d):
        to = (x + 1 + 2 * d) % 4
        return copy_to(spot, spot, send.at[9 + i], recv.at[9 + i], z, 16 * to + 2 * y + c)

    slabs = [x_move(slab(x, 192 * p, 192), 2 * d + p, d) for p, d in ((0, 0), (1, 1), (1, 0), (0, 1))]
    for r in slabs:
        r.start()
    deal_start(r_ref, dealt, d_send, d_recv, z, w, 28, 46)
    for d in range(2):
        slabs[d].wait_recv()
        on = x_move(slab((x + 3 + 2 * d) % 4, 192 * d, 192), 4 + d, d)
        on.start()
        slabs.append(on)
    deal_start(r_ref, dealt, d_send, d_recv, z, w, 46, 64)
    for r in slabs[2:]:
        r.wait_recv()
    half = x_ref.at[:, pl.ds(pl.multiple_of(256 * c, 128), 256)]
    last = copy_to(half, half, send.at[15], recv.at[15], z, 16 * x + 2 * y + (1 - c))
    last.start()
    last.wait()
    for r in rounds + slabs:
        r.wait_send()
    deal_wait(r_ref, dealt, d_send, d_recv, z, w)
    for h in range(2):
        either_wait_send(t_ref.at[h], landed.at[e], send.at[h], recv.at[e], z, w, *homes[h])


def gather_tokens(tokens, rows):
    e = lax.axis_index("wid") % 2
    wide = jnp.pad(tokens, ((0, 0), (0, 64)))
    wide = jnp.where(e == 0, wide, jnp.roll(wide, 64, axis=1)).reshape(2, 96, 128)
    return pl.pallas_call(
        tokens_kernel,
        out_shape=(jax.ShapeDtypeStruct((1536, 512), BF16), jax.ShapeDtypeStruct(rows.shape, BF16)),
        in_specs=[pl.BlockSpec(memory_space=pltpu.VMEM)] * 2,
        out_specs=[pl.BlockSpec(memory_space=pltpu.VMEM)] * 2,
        scratch_shapes=[
            pltpu.VMEM((2, 96, 128), BF16),
            pltpu.VMEM((96, 128), BF16),
            pltpu.SemaphoreType.DMA((16,)),
            pltpu.SemaphoreType.DMA((16,)),
            pltpu.SemaphoreType.DMA,
            pltpu.SemaphoreType.DMA((64,)),
            pltpu.SemaphoreType.DMA((64,)),
        ],
        compiler_params=pltpu.CompilerParams(
            collective_id=0, has_side_effects=True, vmem_limit_bytes=VMEM_BYTES
        ),
        name="gather_tokens",
    )(wide, rows)


def silu(v):
    return v / (1.0 + jnp.exp(-v))


def ring_sum(x_ref, w_ref, got, sent, acc, send, recv, z, w, toward, beside):
    def product(owner, g):
        return lax.dot_general(
            w_ref[owner],
            x_ref[pl.ds(pl.multiple_of(384 * g, 128), 384), :],
            (((1,), (1,)), ((), ())),
            preferred_element_type=F32,
        )

    def hop(d, s, g):
        return copy_to(
            sent.at[d, s, g], got.at[d, s, g], send.at[d, s, g], recv.at[d, s, g], toward[d], w
        )

    def pass_on(d, s, g, add):
        owner = (z + 4 - s) % 8 if d == 0 else (z + 4 + s) % 8
        value = product(owner, g)
        if add:
            hop(d, s - 1, g).wait_recv()
            value = value + got[d, s - 1, g].astype(F32)
        sent[d, s, g] = value.astype(BF16)
        hop(d, s, g).start()

    @pl.loop(0, 2)
    def _(g):
        pass_on(0, 0, g, False)
        pass_on(1, 0, g + 2, False)

    beside(0)

    @pl.loop(0, 2)
    def _(g):
        pass_on(0, 1, g + 2, False)
        pass_on(1, 1, g, False)

    @pl.loop(0, 2)
    def _(g):
        pass_on(0, 1, g, True)
        pass_on(1, 1, g + 2, True)

    beside(1)

    for s in (2, 3):

        @pl.loop(0, 4)
        def _(g):
            pass_on(0, s, (g + 2) % 4, True)
            pass_on(1, s, g, True)

        beside(s)

    @pl.loop(0, 4)
    def _(g):
        acc[g] = product(z, g)

    @pl.loop(0, 4)
    def _(g):
        hop(0, 3, g).wait_recv()
        hop(1, 3, g).wait_recv()
        acc[g] = acc[g] + got[0, 3, g].astype(F32) + got[1, 3, g].astype(F32)

    def finish():
        @pl.loop(0, 2)
        def _(g):
            hop(0, 0, g).wait_send()
            hop(1, 0, g + 2).wait_send()

        for s in (1, 2, 3):

            @pl.loop(0, 4)
            def _(g):
                hop(0, s, g).wait_send()
                hop(1, s, g).wait_send()

    return finish


RING_SCRATCH = [
    pltpu.VMEM((2, 4, GROUPS, 128, 384), BF16),
    pltpu.VMEM((2, 4, GROUPS, 128, 384), BF16),
    pltpu.SemaphoreType.DMA((2, 4, GROUPS)),
    pltpu.SemaphoreType.DMA((2, 4, GROUPS)),
]


def hidden_kernel(
    x_ref, w_ref, r_ref, out_ref, dealt, got, sent, send, recv, acc, hid, ag_send, ag_recv, d_send, d_recv
):
    z, w, _, _, _ = position()
    toward = ((z + 1) % 8, (z + 7) % 8)
    barrier = pltpu.get_barrier_semaphore()
    for n in toward:
        signal(barrier, n, w)
    greet_plane(barrier, z, w)
    pl.semaphore_wait(barrier, 65)
    pltpu.make_async_copy(r_ref.at[w], dealt.at[w], d_recv.at[0]).start()

    def beside(step):
        bounds = (1, 17, 33, 49, 64)
        deal_start(r_ref, dealt, d_send, d_recv, z, w, bounds[step], bounds[step + 1])

    finish = ring_sum(x_ref, w_ref, got, sent, acc, send, recv, z, w, toward, beside)

    @pl.loop(0, 4)
    def _(g):
        gate_a, up_a, gate_b, up_b = (acc[g, 32 * i : 32 * i + 32] for i in range(4))
        hid[0, g] = silu(gate_a) * up_a
        hid[1, g] = silu(gate_b) * up_b
        hid[2, g] = silu(0.5 * (gate_a + gate_b)) * (0.5 * (up_a + up_b))

    def stats(i):
        center = sum(jnp.sum(hid[i, g], axis=1, keepdims=True) for g in range(GROUPS)) / 1536.0
        spread = (
            sum(jnp.sum((hid[i, g] - center) ** 2, axis=1, keepdims=True) for g in range(GROUPS)) / 1536.0
        )
        return center, jnp.sqrt(spread + 1e-05)

    center_a, dev_a = stats(0)
    center_b, dev_b = stats(1)
    center_m, dev_m = stats(2)
    target_std = 0.5 * (dev_a + dev_b)
    target_mean = 0.5 * (center_a + center_b)
    for g in range(GROUPS):
        repaired = (hid[2, g] - center_m) / dev_m * target_std + target_mean
        out_ref[z, :, 384 * g : 384 * g + 384] = repaired.astype(BF16)

    def lap(d, s, h):
        slot = (z + 8 - s) % 8 if d == 0 else (z + s) % 8
        spot = out_ref.at[slot, :, pl.ds(768 * h, 768)]
        return copy_to(spot, spot, ag_send.at[d, s, h], ag_recv.at[d, s, h], toward[d], w)

    def arrived(d, s, h):
        slot = (z + 7 - s) % 8 if d == 0 else (z + 1 + s) % 8
        spot = out_ref.at[slot, :, pl.ds(768 * h, 768)]
        copy_to(spot, spot, ag_send.at[d, s, h], ag_recv.at[d, s, h], toward[d], w).wait_recv()

    laps = []
    for s in range(4):
        for i in range(2):
            for d in range(2):
                h = i if d == 0 else 1 - i
                if s == 3 and i == 1:
                    continue
                if s > 0:
                    arrived(d, s - 1, h)
                one = lap(d, s, h)
                one.start()
                laps.append(one)
    for d in range(2):
        arrived(d, 3, d)
        arrived(d, 2, 1 - d)
    for one in laps:
        one.wait_send()
    finish()
    deal_wait(r_ref, dealt, d_send, d_recv, z, w)


def hidden(x, weights, rows):
    return pl.pallas_call(
        hidden_kernel,
        out_shape=(jax.ShapeDtypeStruct((8, 32, 1536), BF16), jax.ShapeDtypeStruct(rows.shape, BF16)),
        in_specs=[pl.BlockSpec(memory_space=pltpu.VMEM)] * 3,
        out_specs=[pl.BlockSpec(memory_space=pltpu.VMEM)] * 2,
        scratch_shapes=RING_SCRATCH
        + [
            pltpu.VMEM((GROUPS, 128, 384), F32),
            pltpu.VMEM((3, GROUPS, 32, 384), F32),
            pltpu.SemaphoreType.DMA((2, 4, 2)),
            pltpu.SemaphoreType.DMA((2, 4, 2)),
            pltpu.SemaphoreType.DMA((64,)),
            pltpu.SemaphoreType.DMA((64,)),
        ],
        compiler_params=pltpu.CompilerParams(
            collective_id=1, has_side_effects=True, vmem_limit_bytes=VMEM_BYTES
        ),
        name="hidden",
    )(x, weights, rows)


def merge_kernel(
    h_ref, own_w, other_w, out_ref, own_ref, other_ref, c_got, far_sent, far_got, near_sent, near_got, y_own, y_got, final, send, recv
):
    z, w, x, y, c = position()
    q, m = piece_of(x, y, c)
    h = q % 2
    barrier = pltpu.get_barrier_semaphore()
    homes = [piece_home(z, w, i) for i in range(2)]
    targets = [(q // 2, 8 * z + 2 * m + s) for s in range(2)]
    greet(barrier, z, w, x, y, c, homes)
    order = (2, 1, 3, 0)
    swaps = []
    for k in order:
        at = (x + k) % 4
        other_ref[at] = jnp.dot(h_ref[at], other_w[...], preferred_element_type=F32)
        swap = copy_to(
            other_ref.at[at], c_got.at[at], send.at[k], recv.at[k], z, 16 * x + 2 * y + (1 - c)
        )
        swap.start()
        swaps.append(swap)

    for k in order:
        at = (x + k) % 4
        own_ref[at] = jnp.dot(h_ref[at], own_w[...], preferred_element_type=F32)

    def x_move(src, dst, i, d):
        to = (x + 1 + 2 * d) % 4
        return copy_to(src, dst, send.at[4 + i], recv.at[4 + i], z, 16 * to + 2 * y + c)

    moves = []
    swaps[0].wait_recv()
    at = (x + 2) % 4
    for d in range(2):
        rows = slice(192 * d, 192 * d + 192)
        far_sent[d] = (own_ref[at, rows] + c_got[at, rows]).astype(BF16)
        move = x_move(far_sent.at[d], far_got.at[d], d, d)
        move.start()
        moves.append(move)
    for d in range(2):
        at = (x + 1 + 2 * d) % 4
        swaps[1 + d].wait_recv()
        for part in (1 - d, d):
            rows = slice(192 * part, 192 * part + 192)
            value = own_ref[at, rows] + c_got[at, rows]
            if part == d:
                moves[d].wait_recv()
                value = value + far_got[d].astype(F32)
            near_sent[d, part] = value.astype(BF16)
            move = x_move(near_sent.at[d, part], near_got.at[d, part], 2 + 2 * d + part, d)
            move.start()
            moves.append(move)
    swaps[3].wait_recv()
    for move in moves[2:]:
        move.wait_recv()
    for r in range(4):
        for l in range(2):
            rows, lanes = slice(96 * r, 96 * r + 96), slice(128 * l, 128 * l + 128)
            inner = slice(96 * (r % 2), 96 * (r % 2) + 96)
            part = own_ref[x, rows, lanes] + c_got[x, rows, lanes]
            for d in range(2):
                part = part + near_got[d, r // 2, inner, lanes].astype(F32)
            y_own[2 * r + l] = part
    for k in (4, 3, 5, 2, 6, 1, 7):
        at = (y + k) % 8
        move = copy_to(
            y_own.at[at], y_got.at[k - 1], send.at[9 + k], recv.at[9 + k], z, 16 * x + 2 * at + c
        )
        move.start()
        moves.append(move)
    for move in moves[6:]:
        move.wait_recv()
    part = y_own[y]
    for k in range(7):
        part = part + y_got[k]
    final[...] = part.astype(BF16)
    for s in range(2):
        either_start(final, out_ref.at[h], send.at[17 + s], recv.at[17 + h], z, w, *targets[s])
    for i in range(2):
        copy_to(final, out_ref.at[i], send.at[17], recv.at[17 + i], z, w).wait_recv()
    for s in range(2):
        either_wait_send(final, out_ref.at[h], send.at[17 + s], recv.at[17 + h], z, w, *targets[s])
    for move in swaps + moves:
        move.wait_send()


def merge(repaired, own, other):
    return pl.pallas_call(
        merge_kernel,
        out_shape=jax.ShapeDtypeStruct((2, 96, 128), BF16),
        in_specs=[pl.BlockSpec(memory_space=pltpu.VMEM)] * 3,
        out_specs=pl.BlockSpec(memory_space=pltpu.VMEM),
        scratch_shapes=[
            pltpu.VMEM((4, 384, 256), F32),
            pltpu.VMEM((4, 384, 256), F32),
            pltpu.VMEM((4, 384, 256), F32),
            pltpu.VMEM((2, 192, 256), BF16),
            pltpu.VMEM((2, 192, 256), BF16),
            pltpu.VMEM((2, 2, 192, 256), BF16),
            pltpu.VMEM((2, 2, 192, 256), BF16),
            pltpu.VMEM((8, 96, 128), F32),
            pltpu.VMEM((7, 96, 128), F32),
            pltpu.VMEM((96, 128), BF16),
            pltpu.SemaphoreType.DMA((19,)),
            pltpu.SemaphoreType.DMA((19,)),
        ],
        compiler_params=pltpu.CompilerParams(
            collective_id=2, has_side_effects=True, vmem_limit_bytes=VMEM_BYTES
        ),
        name="merge",
    )(repaired, own, other)


def by_dest(*matrices):
    n = len(matrices)
    return jnp.stack(matrices).reshape(n, 2, 64, 2, 512).transpose(2, 0, 1, 3, 4)


def by_block(dealt):
    n = dealt.shape[1]
    return dealt.transpose(1, 0, 2, 3, 4).reshape(n, NB, 2, 512)


def local(tokens, gate_a, up_a, gate_b, up_b, down_a, down_b, block_perm):
    c = lax.axis_index("wid") % 2
    take = functools.partial(jnp.take, indices=block_perm, mode="clip")
    x, rows = gather_tokens(tokens, by_dest(gate_a, up_a, gate_b, up_b))
    rows = by_block(rows)
    weights = jnp.stack((rows[0], rows[1], take(rows[2], axis=0), take(rows[3], axis=0)))
    weights = weights.reshape(4, 8, 32, 512).transpose(1, 0, 2, 3).reshape(8, 128, 512)
    repaired, rows = hidden(x, weights, by_dest(down_a, down_b))
    repaired = repaired.reshape(256, 1536)
    rows = by_block(rows)
    down_mid = ((rows[0].astype(F32) + take(rows[1], axis=0).astype(F32)) * 0.5).astype(BF16).reshape(256, 512)

    halves = (down_mid[:, :256], down_mid[:, 256:])
    own = jnp.where(c == 0, *halves)
    other = jnp.where(c == 0, *halves[::-1])
    merged = merge(repaired.T.reshape(4, 384, 256), own, other).reshape(192, 128)
    return jnp.where(c == 0, merged[:, :64], merged[:, 64:])


def solution(mesh):
    return jax.shard_map(
        local,
        mesh=mesh,
        in_specs=(
            P("tok", "wid"),
            P("wid", "tok"),
            P("wid", "tok"),
            P("wid", "tok"),
            P("wid", "tok"),
            P("wid", "tok"),
            P("wid", "tok"),
            P(),
        ),
        out_specs=P("tok", "wid"),
        check_vma=False,
    )
```

```python
import functools

import jax
import jax.numpy as jnp
from jax import lax
from jax.experimental import pallas as pl
from jax.experimental.pallas import tpu as pltpu
from jax.sharding import PartitionSpec as P

NB = 128
GROUPS = 4
F32 = jnp.float32
BF16 = jnp.bfloat16
MESH_IDS = pl.DeviceIdType.MESH
VMEM_BYTES = 56 * 1024 * 1024


def copy_to(src, dst, send, recv, z, w):
    return pltpu.make_async_remote_copy(
        src_ref=src, dst_ref=dst, send_sem=send, recv_sem=recv, device_id=(z, w), device_id_type=MESH_IDS
    )


def signal(sem, z, w):
    pl.semaphore_signal(sem, inc=1, device_id=(z, w), device_id_type=MESH_IDS)


def position():
    z, w = lax.axis_index("tok"), lax.axis_index("wid")
    return z, w, w // 16, (w // 2) % 8, w % 2


def piece_of(x, y, c):
    return 4 * x + y // 2, 2 * c + y % 2


def piece_home(z, w, h):
    m = (w % 8) // 2
    return w // 8, 4 * (2 * z + h) + 2 * (m % 2) + m // 2


def greet(barrier, z, w, x, y, c, others):
    for k in range(1, 8):
        signal(barrier, z, 16 * x + 2 * ((y + k) % 8) + c)
    for k in range(1, 4):
        signal(barrier, z, 16 * ((x + k) % 4) + 2 * y + c)
    signal(barrier, z, 16 * x + 2 * y + (1 - c))
    greet_others(barrier, z, w, others, 11)


def greet_others(barrier, z, w, others, already):
    own = 0
    for oz, ow in others:
        same = jnp.logical_and(oz == z, ow == w)
        own = own + same.astype(jnp.int32)

        @pl.when(jnp.logical_not(same))
        def _():
            signal(barrier, oz, ow)

    pl.semaphore_wait(barrier, already + len(others) - own)


def either_start(src, dst, send, recv, z, w, oz, ow):
    same = jnp.logical_and(oz == z, ow == w)

    @pl.when(same)
    def _():
        pltpu.make_async_copy(src, dst, recv).start()

    @pl.when(jnp.logical_not(same))
    def _():
        copy_to(src, dst, send, recv, oz, ow).start()


def either_wait_send(src, dst, send, recv, z, w, oz, ow):
    same = jnp.logical_and(oz == z, ow == w)

    @pl.when(jnp.logical_not(same))
    def _():
        copy_to(src, dst, send, recv, oz, ow).wait_send()


def deal(src, dst, send, recv, z, w, low, high, act):
    @pl.loop(low, high)
    def _(k):
        to = (w + k) % 64
        act(copy_to(src.at[to], dst.at[w], send.at[k], recv.at[k], z, to))


def deal_start(src, dst, send, recv, z, w, low, high):
    deal(src, dst, send, recv, z, w, low, high, lambda one: one.start())


def deal_wait(src, dst, send, recv, z, w):
    pltpu.make_async_copy(src.at[w], dst.at[w], recv.at[0]).wait()
    deal(src, dst, send, recv, z, w, 1, 64, lambda one: one.wait())


def greet_plane(barrier, z, w):
    @pl.loop(1, 64)
    def _(k):
        signal(barrier, z, (w + k) % 64)


def tokens_kernel(t_ref, r_ref, x_ref, dealt, landed, piece, send, recv, local_sem, d_send, d_recv):
    z, w, x, y, c = position()
    q, m = piece_of(x, y, c)
    e = w % 2
    barrier = pltpu.get_barrier_semaphore()
    sources = [(q // 2, 8 * z + 2 * m + s) for s in range(2)]
    homes = [piece_home(z, w, h) for h in range(2)]
    greet_plane(barrier, z, w)
    greet_others(barrier, z, w, sources, 63)
    for h in range(2):
        either_start(t_ref.at[h], landed.at[e], send.at[h], recv.at[e], z, w, *homes[h])
    pltpu.make_async_copy(r_ref.at[w], dealt.at[w], d_recv.at[0]).start()
    deal_start(r_ref, dealt, d_send, d_recv, z, w, 1, 12)
    for s in range(2):
        copy_to(t_ref.at[0], landed.at[s], send.at[0], recv.at[s], z, w).wait_recv()
    piece[...] = landed[0] + landed[1]
    spot = x_ref.at[pl.ds(pl.multiple_of(96 * q, 32), 96), pl.ds(pl.multiple_of(128 * m, 128), 128)]
    keep = pltpu.make_async_copy(piece, spot, local_sem)
    keep.start()
    rounds = [
        copy_to(piece, spot, send.at[1 + k], recv.at[1 + k], z, 16 * x + 2 * ((y + k) % 8) + c)
        for k in (4, 3, 5, 2, 6, 1, 7)
    ]
    for r in rounds:
        r.start()
    deal_start(r_ref, dealt, d_send, d_recv, z, w, 12, 28)
    keep.wait()
    for r in rounds:
        r.wait_recv()
    lanes = pl.ds(pl.multiple_of(256 * c, 128), 256)

    def slab(xs, start, size):
        return x_ref.at[pl.ds(pl.multiple_of(384 * xs + start, 64), size), lanes]

    def x_move(spot, i, d):
        to = (x + 1 + 2 * d) % 4
        return copy_to(spot, spot, send.at[9 + i], recv.at[9 + i], z, 16 * to + 2 * y + c)

    slabs = [x_move(slab(x, 192 * p, 192), 2 * d + p, d) for p, d in ((0, 0), (1, 1), (1, 0), (0, 1))]
    for r in slabs:
        r.start()
    deal_start(r_ref, dealt, d_send, d_recv, z, w, 28, 46)
    for d in range(2):
        slabs[d].wait_recv()
        on = x_move(slab((x + 3 + 2 * d) % 4, 192 * d, 192), 4 + d, d)
        on.start()
        slabs.append(on)
    deal_start(r_ref, dealt, d_send, d_recv, z, w, 46, 64)
    for r in slabs[2:]:
        r.wait_recv()
    half = x_ref.at[:, pl.ds(pl.multiple_of(256 * c, 128), 256)]
    last = copy_to(half, half, send.at[15], recv.at[15], z, 16 * x + 2 * y + (1 - c))
    last.start()
    last.wait()
    for r in rounds + slabs:
        r.wait_send()
    deal_wait(r_ref, dealt, d_send, d_recv, z, w)
    for h in range(2):
        either_wait_send(t_ref.at[h], landed.at[e], send.at[h], recv.at[e], z, w, *homes[h])


def gather_tokens(tokens, rows):
    e = lax.axis_index("wid") % 2
    wide = jnp.pad(tokens, ((0, 0), (0, 64)))
    wide = jnp.where(e == 0, wide, jnp.roll(wide, 64, axis=1)).reshape(2, 96, 128)
    return pl.pallas_call(
        tokens_kernel,
        out_shape=(jax.ShapeDtypeStruct((1536, 512), BF16), jax.ShapeDtypeStruct(rows.shape, BF16)),
        in_specs=[pl.BlockSpec(memory_space=pltpu.VMEM)] * 2,
        out_specs=[pl.BlockSpec(memory_space=pltpu.VMEM)] * 2,
        scratch_shapes=[
            pltpu.VMEM((2, 96, 128), BF16),
            pltpu.VMEM((96, 128), BF16),
            pltpu.SemaphoreType.DMA((16,)),
            pltpu.SemaphoreType.DMA((16,)),
            pltpu.SemaphoreType.DMA,
            pltpu.SemaphoreType.DMA((64,)),
            pltpu.SemaphoreType.DMA((64,)),
        ],
        compiler_params=pltpu.CompilerParams(
            collective_id=0, has_side_effects=True, vmem_limit_bytes=VMEM_BYTES
        ),
        name="gather_tokens",
    )(wide, rows)


def silu(v):
    return v / (1.0 + jnp.exp(-v))


def ring_sum(x_ref, w_ref, got, sent, acc, send, recv, z, w, toward, beside, use):
    def product(owner, g):
        return lax.dot_general(
            w_ref[owner],
            x_ref[pl.ds(pl.multiple_of(384 * g, 128), 384), :],
            (((1,), (1,)), ((), ())),
            preferred_element_type=F32,
        )

    def hop(d, s, g):
        return copy_to(
            sent.at[d, s, g], got.at[d, s, g], send.at[d, s, g], recv.at[d, s, g], toward[d], w
        )

    def pass_on(d, s, g, add):
        owner = (z + 4 - s) % 8 if d == 0 else (z + 4 + s) % 8
        value = product(owner, g)
        if add:
            hop(d, s - 1, g).wait_recv()
            value = value + got[d, s - 1, g].astype(F32)
        sent[d, s, g] = value.astype(BF16)
        hop(d, s, g).start()

    @pl.loop(0, 2)
    def _(g):
        pass_on(0, 0, g, False)
        pass_on(1, 0, g + 2, False)

    beside(0)

    @pl.loop(0, 2)
    def _(g):
        pass_on(0, 1, g + 2, False)
        pass_on(1, 1, g, False)

    @pl.loop(0, 2)
    def _(g):
        pass_on(0, 1, g, True)
        pass_on(1, 1, g + 2, True)

    beside(1)

    for s in (2, 3):

        @pl.loop(0, 4)
        def _(g):
            pass_on(0, s, (g + 2) % 4, True)
            pass_on(1, s, g, True)

        beside(s)

    @pl.loop(0, 4)
    def _(g):
        acc[g] = product(z, g)

    @pl.loop(0, 4)
    def _(g):
        hop(0, 3, g).wait_recv()
        hop(1, 3, g).wait_recv()
        use(g, acc[g] + got[0, 3, g].astype(F32) + got[1, 3, g].astype(F32))

    def finish():
        @pl.loop(0, 2)
        def _(g):
            hop(0, 0, g).wait_send()
            hop(1, 0, g + 2).wait_send()

        for s in (1, 2, 3):

            @pl.loop(0, 4)
            def _(g):
                hop(0, s, g).wait_send()
                hop(1, s, g).wait_send()

    return finish


RING_SCRATCH = [
    pltpu.VMEM((2, 4, GROUPS, 128, 384), BF16),
    pltpu.VMEM((2, 4, GROUPS, 128, 384), BF16),
    pltpu.SemaphoreType.DMA((2, 4, GROUPS)),
    pltpu.SemaphoreType.DMA((2, 4, GROUPS)),
]


def hidden_kernel(
    x_ref, w_ref, r_ref, out_ref, dealt, got, sent, send, recv, acc, hid, ag_send, ag_recv, d_send, d_recv
):
    z, w, _, _, _ = position()
    toward = ((z + 1) % 8, (z + 7) % 8)
    barrier = pltpu.get_barrier_semaphore()
    for n in toward:
        signal(barrier, n, w)
    greet_plane(barrier, z, w)
    pl.semaphore_wait(barrier, 65)
    pltpu.make_async_copy(r_ref.at[w], dealt.at[w], d_recv.at[0]).start()

    def beside(step):
        bounds = (1, 17, 33, 49, 64)
        deal_start(r_ref, dealt, d_send, d_recv, z, w, bounds[step], bounds[step + 1])

    def activate(g, total):
        gate_a, up_a, gate_b, up_b = (total[32 * i : 32 * i + 32] for i in range(4))
        hid[0, g] = silu(gate_a) * up_a
        hid[1, g] = silu(gate_b) * up_b
        hid[2, g] = silu(0.5 * (gate_a + gate_b)) * (0.5 * (up_a + up_b))

    finish = ring_sum(x_ref, w_ref, got, sent, acc, send, recv, z, w, toward, beside, activate)

    def stats(i):
        center = sum(jnp.sum(hid[i, g], axis=1, keepdims=True) for g in range(GROUPS)) / 1536.0
        spread = (
            sum(jnp.sum((hid[i, g] - center) ** 2, axis=1, keepdims=True) for g in range(GROUPS)) / 1536.0
        )
        return center, jnp.sqrt(spread + 1e-05)

    center_a, dev_a = stats(0)
    center_b, dev_b = stats(1)
    center_m, dev_m = stats(2)
    target_std = 0.5 * (dev_a + dev_b)
    target_mean = 0.5 * (center_a + center_b)
    for g in range(GROUPS):
        repaired = (hid[2, g] - center_m) / dev_m * target_std + target_mean
        out_ref[z, :, 384 * g : 384 * g + 384] = repaired.astype(BF16)

    def lap(d, s, h):
        slot = (z + 8 - s) % 8 if d == 0 else (z + s) % 8
        spot = out_ref.at[slot, :, pl.ds(384 * h, 384)]
        return copy_to(spot, spot, ag_send.at[d, s, h], ag_recv.at[d, s, h], toward[d], w)

    def arrived(d, s, h):
        slot = (z + 7 - s) % 8 if d == 0 else (z + 1 + s) % 8
        spot = out_ref.at[slot, :, pl.ds(384 * h, 384)]
        copy_to(spot, spot, ag_send.at[d, s, h], ag_recv.at[d, s, h], toward[d], w).wait_recv()

    laps = []
    for s in range(4):
        for i in range(4):
            for d in range(2):
                h = i if d == 0 else (i + 2) % 4
                if s == 3 and i > 1:
                    continue
                if s > 0:
                    arrived(d, s - 1, h)
                one = lap(d, s, h)
                one.start()
                laps.append(one)
    for d in range(2):
        for i in range(2):
            arrived(d, 3, 2 * d + i)
            arrived(d, 2, 2 * (1 - d) + i)
    for one in laps:
        one.wait_send()
    finish()
    deal_wait(r_ref, dealt, d_send, d_recv, z, w)


def hidden(x, weights, rows):
    return pl.pallas_call(
        hidden_kernel,
        out_shape=(jax.ShapeDtypeStruct((8, 32, 1536), BF16), jax.ShapeDtypeStruct(rows.shape, BF16)),
        in_specs=[pl.BlockSpec(memory_space=pltpu.VMEM)] * 3,
        out_specs=[pl.BlockSpec(memory_space=pltpu.VMEM)] * 2,
        scratch_shapes=RING_SCRATCH
        + [
            pltpu.VMEM((GROUPS, 128, 384), F32),
            pltpu.VMEM((3, GROUPS, 32, 384), F32),
            pltpu.SemaphoreType.DMA((2, 4, GROUPS)),
            pltpu.SemaphoreType.DMA((2, 4, GROUPS)),
            pltpu.SemaphoreType.DMA((64,)),
            pltpu.SemaphoreType.DMA((64,)),
        ],
        compiler_params=pltpu.CompilerParams(
            collective_id=1, has_side_effects=True, vmem_limit_bytes=VMEM_BYTES
        ),
        name="hidden",
    )(x, weights, rows)


def merge_kernel(
    h_ref, own_w, other_w, out_ref, own_ref, other_ref, c_got, far_sent, far_got, near_sent, near_got, y_own, y_sent, y_got, final, send, recv, y_send, y_recv
):
    z, w, x, y, c = position()
    q, m = piece_of(x, y, c)
    h = q % 2
    barrier = pltpu.get_barrier_semaphore()
    homes = [piece_home(z, w, i) for i in range(2)]
    targets = [(q // 2, 8 * z + 2 * m + s) for s in range(2)]
    greet(barrier, z, w, x, y, c, homes)
    order = (2, 1, 3, 0)
    swaps = []
    for k in order:
        at = (x + k) % 4
        other_ref[at] = jnp.dot(h_ref[at], other_w[...], preferred_element_type=F32)
        swap = copy_to(
            other_ref.at[at], c_got.at[at], send.at[k], recv.at[k], z, 16 * x + 2 * y + (1 - c)
        )
        swap.start()
        swaps.append(swap)

    for k in order:
        at = (x + k) % 4
        own_ref[at] = jnp.dot(h_ref[at], own_w[...], preferred_element_type=F32)

    def x_move(src, dst, i, d):
        to = (x + 1 + 2 * d) % 4
        return copy_to(src, dst, send.at[4 + i], recv.at[4 + i], z, 16 * to + 2 * y + c)

    moves = []
    swaps[0].wait_recv()
    at = (x + 2) % 4
    for d in range(2):
        rows = slice(192 * d, 192 * d + 192)
        far_sent[d] = (own_ref[at, rows] + c_got[at, rows]).astype(BF16)
        move = x_move(far_sent.at[d], far_got.at[d], d, d)
        move.start()
        moves.append(move)
    for d in range(2):
        at = (x + 1 + 2 * d) % 4
        swaps[1 + d].wait_recv()
        for part in (1 - d, d):
            rows = slice(192 * part, 192 * part + 192)
            value = own_ref[at, rows] + c_got[at, rows]
            if part == d:
                moves[d].wait_recv()
                value = value + far_got[d].astype(F32)
            near_sent[d, part] = value.astype(BF16)
            move = x_move(near_sent.at[d, part], near_got.at[d, part], 2 + 2 * d + part, d)
            move.start()
            moves.append(move)
    swaps[3].wait_recv()
    for move in moves[2:]:
        move.wait_recv()
    for r in range(4):
        for l in range(2):
            rows, lanes = slice(96 * r, 96 * r + 96), slice(128 * l, 128 * l + 128)
            inner = slice(96 * (r % 2), 96 * (r % 2) + 96)
            part = own_ref[x, rows, lanes] + c_got[x, rows, lanes]
            for d in range(2):
                part = part + near_got[d, r // 2, inner, lanes].astype(F32)
            y_own[2 * r + l] = part

    def y_hop(d, step, p):
        to = (y + 1 + 6 * d) % 8
        return copy_to(
            y_sent.at[d, step, p], y_got.at[d, step, p], y_send.at[d, step, p], y_recv.at[d, step, p],
            z, 16 * x + 2 * to + c,
        )

    for step in range(4):
        for far in (False, True):
            for d in range(2):
                p = d if far else 1 - d
                if step == 0 and not far:
                    continue
                owner = (y + 4 - step) % 8 if d == 0 else (y + 4 + step) % 8
                value = y_own[owner, 48 * p : 48 * p + 48]
                if step > (0 if far else 1):
                    y_hop(d, step - 1, p).wait_recv()
                    value = value + y_got[d, step - 1, p]
                y_sent[d, step, p] = value
                move = y_hop(d, step, p)
                move.start()
                moves.append(move)
    for p in range(2):
        part = y_own[y, 48 * p : 48 * p + 48]
        for d in range(2):
            y_hop(d, 3, p).wait_recv()
            part = part + y_got[d, 3, p]
        final[48 * p : 48 * p + 48] = part.astype(BF16)
    for s in range(2):
        either_start(final, out_ref.at[h], send.at[17 + s], recv.at[17 + h], z, w, *targets[s])
    for i in range(2):
        copy_to(final, out_ref.at[i], send.at[17], recv.at[17 + i], z, w).wait_recv()
    for s in range(2):
        either_wait_send(final, out_ref.at[h], send.at[17 + s], recv.at[17 + h], z, w, *targets[s])
    for move in swaps + moves:
        move.wait_send()


def merge(repaired, own, other):
    return pl.pallas_call(
        merge_kernel,
        out_shape=jax.ShapeDtypeStruct((2, 96, 128), BF16),
        in_specs=[pl.BlockSpec(memory_space=pltpu.VMEM)] * 3,
        out_specs=pl.BlockSpec(memory_space=pltpu.VMEM),
        scratch_shapes=[
            pltpu.VMEM((4, 384, 256), F32),
            pltpu.VMEM((4, 384, 256), F32),
            pltpu.VMEM((4, 384, 256), F32),
            pltpu.VMEM((2, 192, 256), BF16),
            pltpu.VMEM((2, 192, 256), BF16),
            pltpu.VMEM((2, 2, 192, 256), BF16),
            pltpu.VMEM((2, 2, 192, 256), BF16),
            pltpu.VMEM((8, 96, 128), F32),
            pltpu.VMEM((2, 4, 2, 48, 128), F32),
            pltpu.VMEM((2, 4, 2, 48, 128), F32),
            pltpu.VMEM((96, 128), BF16),
            pltpu.SemaphoreType.DMA((19,)),
            pltpu.SemaphoreType.DMA((19,)),
            pltpu.SemaphoreType.DMA((2, 4, 2)),
            pltpu.SemaphoreType.DMA((2, 4, 2)),
        ],
        compiler_params=pltpu.CompilerParams(
            collective_id=2, has_side_effects=True, vmem_limit_bytes=VMEM_BYTES
        ),
        name="merge",
    )(repaired, own, other)


def by_dest(*matrices):
    n = len(matrices)
    return jnp.stack(matrices).reshape(n, 2, 64, 2, 512).transpose(2, 0, 1, 3, 4)


def by_block(dealt):
    n = dealt.shape[1]
    return dealt.transpose(1, 0, 2, 3, 4).reshape(n, NB, 2, 512)


def local(tokens, gate_a, up_a, gate_b, up_b, down_a, down_b, block_perm):
    c = lax.axis_index("wid") % 2
    take = functools.partial(jnp.take, indices=block_perm, mode="clip")
    x, rows = gather_tokens(tokens, by_dest(gate_a, up_a, gate_b, up_b))
    rows = by_block(rows)
    weights = jnp.stack((rows[0], rows[1], take(rows[2], axis=0), take(rows[3], axis=0)))
    weights = weights.reshape(4, 8, 32, 512).transpose(1, 0, 2, 3).reshape(8, 128, 512)
    repaired, rows = hidden(x, weights, by_dest(down_a, down_b))
    repaired = repaired.reshape(256, 1536)
    rows = by_block(rows)
    down_mid = ((rows[0].astype(F32) + take(rows[1], axis=0).astype(F32)) * 0.5).astype(BF16).reshape(256, 512)

    halves = (down_mid[:, :256], down_mid[:, 256:])
    own = jnp.where(c == 0, *halves)
    other = jnp.where(c == 0, *halves[::-1])
    merged = merge(repaired.T.reshape(4, 384, 256), own, other).reshape(192, 128)
    return jnp.where(c == 0, merged[:, :64], merged[:, 64:])


def solution(mesh):
    return jax.shard_map(
        local,
        mesh=mesh,
        in_specs=(
            P("tok", "wid"),
            P("wid", "tok"),
            P("wid", "tok"),
            P("wid", "tok"),
            P("wid", "tok"),
            P("wid", "tok"),
            P("wid", "tok"),
            P(),
        ),
        out_specs=P("tok", "wid"),
        check_vma=False,
    )
```

```python
import jax
import jax.numpy as jnp
from jax import lax
from jax.experimental import pallas as pl
from jax.experimental.pallas import tpu as pltpu
from jax.sharding import PartitionSpec as P

NB = 128
GROUPS = 4
F32 = jnp.float32
BF16 = jnp.bfloat16
MESH_IDS = pl.DeviceIdType.MESH
VMEM_BYTES = 56 * 1024 * 1024


def copy_to(src, dst, send, recv, z, w):
    return pltpu.make_async_remote_copy(
        src_ref=src, dst_ref=dst, send_sem=send, recv_sem=recv, device_id=(z, w), device_id_type=MESH_IDS
    )


def signal(sem, z, w):
    pl.semaphore_signal(sem, inc=1, device_id=(z, w), device_id_type=MESH_IDS)


def position():
    z, w = lax.axis_index("tok"), lax.axis_index("wid")
    return z, w, w // 16, (w // 2) % 8, w % 2


def piece_of(x, y, c):
    return 4 * x + y // 2, 2 * c + y % 2


def piece_home(z, w, h):
    m = (w % 8) // 2
    return w // 8, 4 * (2 * z + h) + 2 * (m % 2) + m // 2


def greet(barrier, z, w, x, y, c, others):
    for k in range(1, 8):
        signal(barrier, z, 16 * x + 2 * ((y + k) % 8) + c)
    for k in range(1, 4):
        signal(barrier, z, 16 * ((x + k) % 4) + 2 * y + c)
    signal(barrier, z, 16 * x + 2 * y + (1 - c))
    greet_others(barrier, z, w, others, 11)


def greet_others(barrier, z, w, others, already):
    own = 0
    for oz, ow in others:
        same = jnp.logical_and(oz == z, ow == w)
        own = own + same.astype(jnp.int32)

        @pl.when(jnp.logical_not(same))
        def _():
            signal(barrier, oz, ow)

    pl.semaphore_wait(barrier, already + len(others) - own)


def either_start(src, dst, send, recv, z, w, oz, ow):
    same = jnp.logical_and(oz == z, ow == w)

    @pl.when(same)
    def _():
        pltpu.make_async_copy(src, dst, recv).start()

    @pl.when(jnp.logical_not(same))
    def _():
        copy_to(src, dst, send, recv, oz, ow).start()


def either_wait_send(src, dst, send, recv, z, w, oz, ow):
    same = jnp.logical_and(oz == z, ow == w)

    @pl.when(jnp.logical_not(same))
    def _():
        copy_to(src, dst, send, recv, oz, ow).wait_send()


def deal(src, dst, send, recv, z, w, low, high, act):
    @pl.loop(low, high)
    def _(k):
        to = (w + k) % 64
        act(copy_to(src.at[to], dst.at[w], send.at[k], recv.at[k], z, to))


def deal_start(src, dst, send, recv, z, w, low, high):
    deal(src, dst, send, recv, z, w, low, high, lambda one: one.start())


def deal_wait(src, dst, send, recv, z, w):
    pltpu.make_async_copy(src.at[w], dst.at[w], recv.at[0]).wait()
    deal(src, dst, send, recv, z, w, 1, 64, lambda one: one.wait())


def greet_plane(barrier, z, w):
    @pl.loop(1, 64)
    def _(k):
        signal(barrier, z, (w + k) % 64)


def tokens_kernel(t_ref, r_ref, x_ref, dealt, landed, piece, send, recv, local_sem, d_send, d_recv):
    z, w, x, y, c = position()
    q, m = piece_of(x, y, c)
    e = w % 2
    barrier = pltpu.get_barrier_semaphore()
    sources = [(q // 2, 8 * z + 2 * m + s) for s in range(2)]
    homes = [piece_home(z, w, h) for h in range(2)]
    greet_plane(barrier, z, w)
    greet_others(barrier, z, w, sources, 63)
    for h in range(2):
        either_start(t_ref.at[h], landed.at[e], send.at[h], recv.at[e], z, w, *homes[h])
    pltpu.make_async_copy(r_ref.at[w], dealt.at[w], d_recv.at[0]).start()
    deal_start(r_ref, dealt, d_send, d_recv, z, w, 1, 12)
    for s in range(2):
        copy_to(t_ref.at[0], landed.at[s], send.at[0], recv.at[s], z, w).wait_recv()
    piece[...] = landed[0] + landed[1]
    spot = x_ref.at[pl.ds(pl.multiple_of(96 * q, 32), 96), pl.ds(pl.multiple_of(128 * m, 128), 128)]
    keep = pltpu.make_async_copy(piece, spot, local_sem)
    keep.start()
    rounds = [
        copy_to(piece, spot, send.at[1 + k], recv.at[1 + k], z, 16 * x + 2 * ((y + k) % 8) + c)
        for k in (4, 3, 5, 2, 6, 1, 7)
    ]
    for r in rounds:
        r.start()
    deal_start(r_ref, dealt, d_send, d_recv, z, w, 12, 28)
    keep.wait()
    for r in rounds:
        r.wait_recv()
    lanes = pl.ds(pl.multiple_of(256 * c, 128), 256)

    def slab(xs, start, size):
        return x_ref.at[pl.ds(pl.multiple_of(384 * xs + start, 64), size), lanes]

    def x_move(spot, i, d):
        to = (x + 1 + 2 * d) % 4
        return copy_to(spot, spot, send.at[9 + i], recv.at[9 + i], z, 16 * to + 2 * y + c)

    slabs = [x_move(slab(x, 192 * p, 192), 2 * d + p, d) for p, d in ((0, 0), (1, 1), (1, 0), (0, 1))]
    for r in slabs:
        r.start()
    deal_start(r_ref, dealt, d_send, d_recv, z, w, 28, 46)
    for d in range(2):
        slabs[d].wait_recv()
        on = x_move(slab((x + 3 + 2 * d) % 4, 192 * d, 192), 4 + d, d)
        on.start()
        slabs.append(on)
    deal_start(r_ref, dealt, d_send, d_recv, z, w, 46, 64)
    for r in slabs[2:]:
        r.wait_recv()
    half = x_ref.at[:, pl.ds(pl.multiple_of(256 * c, 128), 256)]
    last = copy_to(half, half, send.at[15], recv.at[15], z, 16 * x + 2 * y + (1 - c))
    last.start()
    last.wait()
    for r in rounds + slabs:
        r.wait_send()
    deal_wait(r_ref, dealt, d_send, d_recv, z, w)
    for h in range(2):
        either_wait_send(t_ref.at[h], landed.at[e], send.at[h], recv.at[e], z, w, *homes[h])


def gather_tokens(tokens, rows):
    e = lax.axis_index("wid") % 2
    wide = jnp.pad(tokens, ((0, 0), (0, 64)))
    wide = jnp.where(e == 0, wide, jnp.roll(wide, 64, axis=1)).reshape(2, 96, 128)
    return pl.pallas_call(
        tokens_kernel,
        out_shape=(jax.ShapeDtypeStruct((1536, 512), BF16), jax.ShapeDtypeStruct(rows.shape, BF16)),
        in_specs=[pl.BlockSpec(memory_space=pltpu.VMEM)] * 2,
        out_specs=[pl.BlockSpec(memory_space=pltpu.VMEM)] * 2,
        scratch_shapes=[
            pltpu.VMEM((2, 96, 128), BF16),
            pltpu.VMEM((96, 128), BF16),
            pltpu.SemaphoreType.DMA((16,)),
            pltpu.SemaphoreType.DMA((16,)),
            pltpu.SemaphoreType.DMA,
            pltpu.SemaphoreType.DMA((64,)),
            pltpu.SemaphoreType.DMA((64,)),
        ],
        compiler_params=pltpu.CompilerParams(
            collective_id=0, has_side_effects=True, vmem_limit_bytes=VMEM_BYTES
        ),
        name="gather_tokens",
    )(wide, rows)


def silu(v):
    return v / (1.0 + jnp.exp(-v))


def ring_sum(x_ref, w_ref, got, sent, acc, send, recv, z, w, toward, beside, use):
    def product(owner, g):
        return lax.dot_general(
            w_ref[owner],
            x_ref[pl.ds(pl.multiple_of(384 * g, 128), 384), :],
            (((1,), (1,)), ((), ())),
            preferred_element_type=F32,
        )

    def hop(d, s, g):
        return copy_to(
            sent.at[d, s, g], got.at[d, s, g], send.at[d, s, g], recv.at[d, s, g], toward[d], w
        )

    def pass_on(d, s, g, add):
        owner = (z + 4 - s) % 8 if d == 0 else (z + 4 + s) % 8
        value = product(owner, g)
        if add:
            hop(d, s - 1, g).wait_recv()
            value = value + got[d, s - 1, g].astype(F32)
        sent[d, s, g] = value.astype(BF16)
        hop(d, s, g).start()

    @pl.loop(0, 2)
    def _(g):
        pass_on(0, 0, g, False)
        pass_on(1, 0, g + 2, False)

    beside(0)

    @pl.loop(0, 2)
    def _(g):
        pass_on(0, 1, g + 2, False)
        pass_on(1, 1, g, False)

    @pl.loop(0, 2)
    def _(g):
        pass_on(0, 1, g, True)
        pass_on(1, 1, g + 2, True)

    beside(1)

    for s in (2, 3):

        @pl.loop(0, 4)
        def _(g):
            pass_on(0, s, (g + 2) % 4, True)
            pass_on(1, s, g, True)

        beside(s)

    @pl.loop(0, 4)
    def _(g):
        acc[g] = product(z, g)

    @pl.loop(0, 4)
    def _(g):
        hop(0, 3, g).wait_recv()
        hop(1, 3, g).wait_recv()
        use(g, acc[g] + got[0, 3, g].astype(F32) + got[1, 3, g].astype(F32))

    def finish():
        @pl.loop(0, 2)
        def _(g):
            hop(0, 0, g).wait_send()
            hop(1, 0, g + 2).wait_send()

        for s in (1, 2, 3):

            @pl.loop(0, 4)
            def _(g):
                hop(0, s, g).wait_send()
                hop(1, s, g).wait_send()

    return finish


RING_SCRATCH = [
    pltpu.VMEM((2, 4, GROUPS, 128, 384), BF16),
    pltpu.VMEM((2, 4, GROUPS, 128, 384), BF16),
    pltpu.SemaphoreType.DMA((2, 4, GROUPS)),
    pltpu.SemaphoreType.DMA((2, 4, GROUPS)),
]


def hidden_kernel(
    x_ref, w_ref, r_ref, out_ref, dealt, got, sent, send, recv, acc, hid, ag_send, ag_recv, d_send, d_recv
):
    z, w, _, _, _ = position()
    toward = ((z + 1) % 8, (z + 7) % 8)
    barrier = pltpu.get_barrier_semaphore()
    for n in toward:
        signal(barrier, n, w)
    greet_plane(barrier, z, w)
    pl.semaphore_wait(barrier, 65)
    pltpu.make_async_copy(r_ref.at[w], dealt.at[w], d_recv.at[0]).start()

    def beside(step):
        bounds = (1, 17, 33, 49, 64)
        deal_start(r_ref, dealt, d_send, d_recv, z, w, bounds[step], bounds[step + 1])

    def activate(g, total):
        gate_a, up_a, gate_b, up_b = (total[32 * i : 32 * i + 32] for i in range(4))
        hid[0, g] = silu(gate_a) * up_a
        hid[1, g] = silu(gate_b) * up_b
        hid[2, g] = silu(0.5 * (gate_a + gate_b)) * (0.5 * (up_a + up_b))

    finish = ring_sum(x_ref, w_ref, got, sent, acc, send, recv, z, w, toward, beside, activate)

    def stats(i):
        center = sum(jnp.sum(hid[i, g], axis=1, keepdims=True) for g in range(GROUPS)) / 1536.0
        spread = (
            sum(jnp.sum((hid[i, g] - center) ** 2, axis=1, keepdims=True) for g in range(GROUPS)) / 1536.0
        )
        return center, jnp.sqrt(spread + 1e-05)

    center_a, dev_a = stats(0)
    center_b, dev_b = stats(1)
    center_m, dev_m = stats(2)
    target_std = 0.5 * (dev_a + dev_b)
    target_mean = 0.5 * (center_a + center_b)
    for g in range(GROUPS):
        repaired = (hid[2, g] - center_m) / dev_m * target_std + target_mean
        out_ref[z, :, 384 * g : 384 * g + 384] = repaired.astype(BF16)

    def lap(d, s, h):
        slot = (z + 8 - s) % 8 if d == 0 else (z + s) % 8
        spot = out_ref.at[slot, :, pl.ds(384 * h, 384)]
        return copy_to(spot, spot, ag_send.at[d, s, h], ag_recv.at[d, s, h], toward[d], w)

    def arrived(d, s, h):
        slot = (z + 7 - s) % 8 if d == 0 else (z + 1 + s) % 8
        spot = out_ref.at[slot, :, pl.ds(384 * h, 384)]
        copy_to(spot, spot, ag_send.at[d, s, h], ag_recv.at[d, s, h], toward[d], w).wait_recv()

    laps = []
    for s in range(4):
        for i in range(4):
            for d in range(2):
                h = i if d == 0 else (i + 2) % 4
                if s == 3 and i > 1:
                    continue
                if s > 0:
                    arrived(d, s - 1, h)
                one = lap(d, s, h)
                one.start()
                laps.append(one)
    for d in range(2):
        for i in range(2):
            arrived(d, 3, 2 * d + i)
            arrived(d, 2, 2 * (1 - d) + i)
    for one in laps:
        one.wait_send()
    finish()
    deal_wait(r_ref, dealt, d_send, d_recv, z, w)


def hidden(x, weights, rows):
    return pl.pallas_call(
        hidden_kernel,
        out_shape=(jax.ShapeDtypeStruct((8, 32, 1536), BF16), jax.ShapeDtypeStruct(rows.shape, BF16)),
        in_specs=[pl.BlockSpec(memory_space=pltpu.VMEM)] * 3,
        out_specs=[pl.BlockSpec(memory_space=pltpu.VMEM)] * 2,
        scratch_shapes=RING_SCRATCH
        + [
            pltpu.VMEM((GROUPS, 128, 384), F32),
            pltpu.VMEM((3, GROUPS, 32, 384), F32),
            pltpu.SemaphoreType.DMA((2, 4, GROUPS)),
            pltpu.SemaphoreType.DMA((2, 4, GROUPS)),
            pltpu.SemaphoreType.DMA((64,)),
            pltpu.SemaphoreType.DMA((64,)),
        ],
        compiler_params=pltpu.CompilerParams(
            collective_id=1, has_side_effects=True, vmem_limit_bytes=VMEM_BYTES
        ),
        name="hidden",
    )(x, weights, rows)


def merge_kernel(
    h_ref, own_w, other_w, out_ref, own_ref, other_ref, c_got, far_sent, far_got, near_sent, near_got, y_own, y_got, final, send, recv
):
    z, w, x, y, c = position()
    q, m = piece_of(x, y, c)
    h = q % 2
    barrier = pltpu.get_barrier_semaphore()
    homes = [piece_home(z, w, i) for i in range(2)]
    targets = [(q // 2, 8 * z + 2 * m + s) for s in range(2)]
    greet(barrier, z, w, x, y, c, homes)
    order = (2, 1, 3, 0)
    swaps = []
    for k in order:
        at = (x + k) % 4
        other_ref[at] = jnp.dot(h_ref[at], other_w[...], preferred_element_type=F32)
        swap = copy_to(
            other_ref.at[at], c_got.at[at], send.at[k], recv.at[k], z, 16 * x + 2 * y + (1 - c)
        )
        swap.start()
        swaps.append(swap)

    for k in order:
        at = (x + k) % 4
        own_ref[at] = jnp.dot(h_ref[at], own_w[...], preferred_element_type=F32)

    def x_move(src, dst, i, d):
        to = (x + 1 + 2 * d) % 4
        return copy_to(src, dst, send.at[4 + i], recv.at[4 + i], z, 16 * to + 2 * y + c)

    moves = []
    swaps[0].wait_recv()
    at = (x + 2) % 4
    for d in range(2):
        rows = slice(192 * d, 192 * d + 192)
        far_sent[d] = (own_ref[at, rows] + c_got[at, rows]).astype(BF16)
        move = x_move(far_sent.at[d], far_got.at[d], d, d)
        move.start()
        moves.append(move)
    for d in range(2):
        at = (x + 1 + 2 * d) % 4
        swaps[1 + d].wait_recv()
        for part in (1 - d, d):
            rows = slice(192 * part, 192 * part + 192)
            value = own_ref[at, rows] + c_got[at, rows]
            if part == d:
                moves[d].wait_recv()
                value = value + far_got[d].astype(F32)
            near_sent[d, part] = value.astype(BF16)
            move = x_move(near_sent.at[d, part], near_got.at[d, part], 2 + 2 * d + part, d)
            move.start()
            moves.append(move)
    swaps[3].wait_recv()
    for move in moves[2:]:
        move.wait_recv()
    for r in range(4):
        for l in range(2):
            rows, lanes = slice(96 * r, 96 * r + 96), slice(128 * l, 128 * l + 128)
            inner = slice(96 * (r % 2), 96 * (r % 2) + 96)
            part = own_ref[x, rows, lanes] + c_got[x, rows, lanes]
            for d in range(2):
                part = part + near_got[d, r // 2, inner, lanes].astype(F32)
            y_own[2 * r + l] = part
    for k in (4, 3, 5, 2, 6, 1, 7):
        at = (y + k) % 8
        move = copy_to(
            y_own.at[at], y_got.at[k - 1], send.at[9 + k], recv.at[9 + k], z, 16 * x + 2 * at + c
        )
        move.start()
        moves.append(move)
    for move in moves[6:]:
        move.wait_recv()
    part = y_own[y]
    for k in range(7):
        part = part + y_got[k]
    final[...] = part.astype(BF16)
    for s in range(2):
        either_start(final, out_ref.at[h], send.at[17 + s], recv.at[17 + h], z, w, *targets[s])
    for i in range(2):
        copy_to(final, out_ref.at[i], send.at[17], recv.at[17 + i], z, w).wait_recv()
    for s in range(2):
        either_wait_send(final, out_ref.at[h], send.at[17 + s], recv.at[17 + h], z, w, *targets[s])
    for move in swaps + moves:
        move.wait_send()


def merge(repaired, own, other):
    return pl.pallas_call(
        merge_kernel,
        out_shape=jax.ShapeDtypeStruct((2, 96, 128), BF16),
        in_specs=[pl.BlockSpec(memory_space=pltpu.VMEM)] * 3,
        out_specs=pl.BlockSpec(memory_space=pltpu.VMEM),
        scratch_shapes=[
            pltpu.VMEM((4, 384, 256), F32),
            pltpu.VMEM((4, 384, 256), F32),
            pltpu.VMEM((4, 384, 256), F32),
            pltpu.VMEM((2, 192, 256), BF16),
            pltpu.VMEM((2, 192, 256), BF16),
            pltpu.VMEM((2, 2, 192, 256), BF16),
            pltpu.VMEM((2, 2, 192, 256), BF16),
            pltpu.VMEM((8, 96, 128), F32),
            pltpu.VMEM((7, 96, 128), F32),
            pltpu.VMEM((96, 128), BF16),
            pltpu.SemaphoreType.DMA((19,)),
            pltpu.SemaphoreType.DMA((19,)),
        ],
        compiler_params=pltpu.CompilerParams(
            collective_id=2, has_side_effects=True, vmem_limit_bytes=VMEM_BYTES
        ),
        name="merge",
    )(repaired, own, other)


def by_dest(*matrices):
    n = len(matrices)
    return jnp.stack(matrices).reshape(n, 2, 64, 2, 512).transpose(2, 0, 1, 3, 4)


def by_block(dealt):
    n = dealt.shape[1]
    return dealt.transpose(1, 0, 2, 3, 4).reshape(n, NB, 2, 512)


def local(tokens, gate_a, up_a, gate_b, up_b, down_a, down_b, block_perm):
    c = lax.axis_index("wid") % 2

    def take(blocks):
        return blocks.at[block_perm].get(mode="promise_in_bounds")

    x, rows = gather_tokens(tokens, by_dest(gate_a, up_a, gate_b, up_b))
    rows = by_block(rows)
    weights = jnp.stack((rows[0], rows[1], take(rows[2]), take(rows[3])))
    weights = weights.reshape(4, 8, 32, 512).transpose(1, 0, 2, 3).reshape(8, 128, 512)
    repaired, rows = hidden(x, weights, by_dest(down_a, down_b))
    repaired = repaired.reshape(256, 1536)
    rows = by_block(rows)
    down_mid = ((rows[0].astype(F32) + take(rows[1]).astype(F32)) * 0.5).astype(BF16).reshape(256, 512)

    halves = (down_mid[:, :256], down_mid[:, 256:])
    own = jnp.where(c == 0, *halves)
    other = jnp.where(c == 0, *halves[::-1])
    merged = merge(repaired.T.reshape(4, 384, 256), own, other).reshape(192, 128)
    return jnp.where(c == 0, merged[:, :64], merged[:, 64:])


def solution(mesh):
    return jax.shard_map(
        local,
        mesh=mesh,
        in_specs=(
            P("tok", "wid"),
            P("wid", "tok"),
            P("wid", "tok"),
            P("wid", "tok"),
            P("wid", "tok"),
            P("wid", "tok"),
            P("wid", "tok"),
            P(),
        ),
        out_specs=P("tok", "wid"),
        check_vma=False,
    )
```
